512 devices in a mesh: inst: 32 (over y, z_lo, core), space: 16 (over z_hi, x).
Axes of the slice: x: 4, y: 4, z: 16 (z_hi: 4, z_lo: 4; z = z_hi * 4 + z_lo), core: 2. Of those that a mesh axis runs over, the one named last changes fastest.
Arguments:
- flow_state: float32 [32, 6, 1024, 128], P('inst', None, 'space'), may hold values from -6 to 6
- forcing: float32 [32, 6, 1024, 128], P('inst', None, 'space'), may hold values from -6 to 6
- pivot_table: float32 [8, 6, 6, 128], replicated, may hold values from -0.21 to 1, as said below
- block_offset: int32 [1024], P('space'), may hold values from 0 to 7
- line_perm: int32 [128], replicated, may hold values from 0 to 127, each once
- axial_jac: float32 [6, 6], replicated, may hold values from -2.5 to 2.5
- radial_jac: float32 [6, 6], replicated, may hold values from -2.5 to 2.5
- lower_block: float32 [6, 6], replicated, may hold values from -0.035 to 0.97, as said below
- upper_block: float32 [6, 6], replicated, may hold values from -0.035 to 0.97, as said below
Outputs:
- residual: float32 [32, 6, 1024, 128], P('inst', None, 'space')
- correction: float32 [32, 6, 1024, 128], P('inst', None, 'space')
The draws below stay inside these ranges and needn't reach their ends.
Inputs may be any that keep to these rules, and one draw needn't show every extreme that they name: `pivot_table`: diagonal entries lie in 0.6 to 1. `lower_block`: diagonal entries lie in 0.3 to 0.97, the others in -0.035 to 0.035. `upper_block`: diagonal entries lie in 0.3 to 0.97, the others in -0.035 to 0.035.
All inputs are finite; a program needn't handle non-finite values.
Results may differ from the reference program's by a relative error of at most 0.0001.
Values sent between devices are 32-bit elements; how exact they have to be, the bound alone decides.
No kernel may reach another device: no remote copies, remote signals or barrier semaphores. Data moves between devices by JAX's collectives and lax.ppermute only.
A program may use at most 64 MiB of HBM per device.

```python
import math
import jax
import jax.numpy as jnp
from jax import lax

NV = 6
NR = 128
KB = 8
NT = 32
NA = 1024


def draw_pivot_table(key, part):
    diag_key, off_key = jax.random.split(jax.random.fold_in(key, 17))
    off_values = 0.07 * jax.random.truncated_normal(off_key, -3.0, 3.0, (KB, NV, NV, NR), jnp.float32)
    diag_values = jnp.exp(jax.random.uniform(diag_key, (KB, NV, 1, NR), jnp.float32, math.log(0.6), math.log(1.0)))
    row_index = lax.broadcasted_iota(jnp.int32, (1, NV, NV, 1), 1)
    col_index = lax.broadcasted_iota(jnp.int32, (1, NV, NV, 1), 2)
    return jnp.where(row_index == col_index, diag_values, off_values)


def draw_lower_block(key, part):
    diag_key, off_key = jax.random.split(jax.random.fold_in(key, 29))
    diag_values = jnp.exp(jax.random.uniform(diag_key, (NV, 1), jnp.float32, math.log(0.3), math.log(0.97)))
    off_values = jax.random.uniform(off_key, (NV, NV), jnp.float32, -0.035, 0.035)
    row_index = lax.broadcasted_iota(jnp.int32, (NV, NV), 0)
    col_index = lax.broadcasted_iota(jnp.int32, (NV, NV), 1)
    return jnp.where(row_index == col_index, diag_values, off_values)


def draw_upper_block(key, part):
    diag_key, off_key = jax.random.split(jax.random.fold_in(key, 43))
    diag_values = jnp.exp(jax.random.uniform(diag_key, (NV, 1), jnp.float32, math.log(0.3), math.log(0.97)))
    off_values = jax.random.uniform(off_key, (NV, NV), jnp.float32, -0.035, 0.035)
    row_index = lax.broadcasted_iota(jnp.int32, (NV, NV), 0)
    col_index = lax.broadcasted_iota(jnp.int32, (NV, NV), 1)
    return jnp.where(row_index == col_index, diag_values, off_values)


def plant(entries, stream_key, low, high):
    index_at = [jax.random.randint(jax.random.fold_in(stream_key, axis), (), 0, length) for axis, length in enumerate(entries.shape)]
    main_axis = entries.shape.index(max(entries.shape))
    next_to = index_at[:main_axis] + [(index_at[main_axis] + 1) % entries.shape[main_axis]] + index_at[main_axis + 1:]
    return entries.at[tuple(index_at)].set(low).at[tuple(next_to)].set(high)


def levels(stream_key, dims, cuts, least, high):
    factor_of, own = 1.0, jax.random.fold_in(stream_key, 6)
    for dim, parts in cuts:
        steps = jnp.exp(jax.random.uniform(jax.random.fold_in(own, dim), (parts,), jnp.float32, least / len(cuts), high / len(cuts)))
        factor_of = factor_of * jnp.repeat(steps, dims[dim] // parts).reshape([-1 if axis == dim else 1 for axis in range(len(dims))])
    return factor_of


def gaussian(key, shape, deviation, reach, cuts=(), dtype=jnp.bfloat16):
    level = levels(key, shape, cuts, -0.22, 0.18) if cuts else 1.0
    result = jax.random.normal(key, shape, jnp.float32) * deviation * level
    return jnp.minimum(jnp.maximum(result, -reach), reach).astype(dtype)


def setup_inputs(seed: int = 0) -> dict:
    arg_keys = jax.random.split(jax.random.key(seed), 10)
    flow_state = gaussian(arg_keys[0], (NT, NV, NA, NR), 1.0, 6.0, ((0, 32), (2, 16)), jnp.float32)
    forcing = gaussian(arg_keys[1], (NT, NV, NA, NR), 1.0, 6.0, ((0, 32), (2, 16)), jnp.float32)
    pivot_table = draw_pivot_table(jax.random.fold_in(arg_keys[9], 71), 0)
    block_offset = plant(jax.random.randint(arg_keys[3], (NA,), 0, KB), jax.random.fold_in(arg_keys[3], 1), 0, KB - 1).astype(jnp.int32)
    line_perm = jax.random.permutation(arg_keys[4], NR).astype(jnp.int32)
    axial_jac = gaussian(arg_keys[5], (NV, NV), NV ** -0.5, 2.5, (), jnp.float32)
    radial_jac = gaussian(arg_keys[6], (NV, NV), NV ** -0.5, 2.5, (), jnp.float32)
    lower_block = draw_lower_block(jax.random.fold_in(arg_keys[9], 71), 0)
    upper_block = draw_upper_block(jax.random.fold_in(arg_keys[9], 71), 0)
    return dict(flow_state=flow_state, forcing=forcing, pivot_table=pivot_table, block_offset=block_offset, line_perm=line_perm, axial_jac=axial_jac, radial_jac=radial_jac, lower_block=lower_block, upper_block=upper_block)


frequency = 0.5
viscosity = 0.01
damping = 0.25


def spectral_matrix(count):
    row_index = lax.broadcasted_iota(jnp.int32, (count, count), 0)
    col_index = lax.broadcasted_iota(jnp.int32, (count, count), 1)
    distance = row_index - col_index
    parity = (1 - 2 * jnp.mod(distance, 2)).astype(jnp.float32)
    phase_angle = jnp.pi * distance.astype(jnp.float32) / count
    diagonal_mask = distance == 0
    sine_value = jnp.where(diagonal_mask, 1.0, jnp.sin(phase_angle))
    first_order = jnp.where(diagonal_mask, 0.0, 0.5 * parity * jnp.cos(phase_angle) / sine_value)
    second_order = jnp.where(diagonal_mask, -(count * count + 2) / 12.0, -0.5 * parity / (sine_value * sine_value))
    return (frequency * first_order - viscosity * second_order).astype(jnp.float32)


def reference(flow_state, forcing, pivot_table, block_offset, line_perm, axial_jac, radial_jac, lower_block, upper_block):
    hp = lax.Precision.HIGHEST
    line_state = jnp.take(flow_state, line_perm, axis=3)
    line_forcing = jnp.take(forcing, line_perm, axis=3)
    spectral = spectral_matrix(NT)
    timed = jnp.einsum('nm,mvar->nvar', spectral, line_state, precision=hp)
    axial_padded = jnp.pad(line_state, ((0, 0), (0, 0), (1, 1), (0, 0)))
    radial_padded = jnp.pad(line_state, ((0, 0), (0, 0), (0, 0), (1, 1)))
    axial_ahead = axial_padded[:, :, 2:]
    axial_behind = axial_padded[:, :, :-2]
    radial_outer = radial_padded[..., 2:]
    radial_inner = radial_padded[..., :-2]
    flux_terms = jnp.einsum('vw,nwar->nvar', axial_jac, 0.5 * (axial_ahead - axial_behind), precision=hp)
    flux_terms = flux_terms + jnp.einsum('vw,nwar->nvar', radial_jac, 0.5 * (radial_outer - radial_inner), precision=hp)
    residual = flux_terms - damping * (axial_ahead + axial_behind + radial_outer + radial_inner - 4.0 * line_state) + timed - line_forcing
    factors = jnp.take(pivot_table, block_offset, axis=0)
    stacked = jnp.transpose(factors, (3, 1, 2, 0))
    residual_lines = jnp.transpose(residual, (3, 0, 1, 2))

    def forward(previous, element):
        factor, target = element
        inside = target - jnp.einsum('vw,nwa->nva', lower_block, previous, precision=hp)
        current = jnp.einsum('vwa,nwa->nva', factor, inside, precision=hp)
        return current, current

    initial = jnp.zeros((NT, NV, NA), jnp.float32)
    _, forward_sweep = lax.scan(forward, initial, (stacked, residual_lines))

    def backward(following, element):
        factor, partial_value = element
        coupled = jnp.einsum('vw,nwa->nva', upper_block, following, precision=hp)
        current = partial_value - jnp.einsum('vwa,nwa->nva', factor, coupled, precision=hp)
        return current, current

    _, backward_sweep = lax.scan(backward, initial, (stacked, forward_sweep), reverse=True)
    correction = jnp.transpose(backward_sweep, (1, 2, 3, 0))
    return residual, correction
```

```python
import jax
import jax.numpy as jnp
from jax import lax
from jax.experimental import pallas as pl
from jax.experimental.pallas import tpu as pltpu
from jax.sharding import PartitionSpec as P

frequency = 0.5
viscosity = 0.01
damping = 0.25

NV = 6
NQ = 8
NS = 8
NH = 2
KB = 8
LANES = 128
LEVELS = 4


def spectral_matrix(count):
    row_index = lax.broadcasted_iota(jnp.int32, (count, count), 0)
    col_index = lax.broadcasted_iota(jnp.int32, (count, count), 1)
    distance = row_index - col_index
    parity = (1 - 2 * jnp.mod(distance, 2)).astype(jnp.float32)
    phase_angle = jnp.pi * distance.astype(jnp.float32) / count
    diagonal_mask = distance == 0
    sine_value = jnp.where(diagonal_mask, 1.0, jnp.sin(phase_angle))
    first_order = jnp.where(diagonal_mask, 0.0, 0.5 * parity * jnp.cos(phase_angle) / sine_value)
    second_order = jnp.where(
        diagonal_mask, -(count * count + 2) / 12.0, -0.5 * parity / (sine_value * sine_value)
    )
    return frequency * first_order - viscosity * second_order


def shift_chunks(tile, amount):
    sub = lax.broadcasted_iota(jnp.int32, tile.shape, 0)
    lane = lax.broadcasted_iota(jnp.int32, tile.shape, 1)
    zero = jnp.zeros_like(tile)
    swapped = pltpu.roll(tile, LANES // 2, 1)
    if amount == NQ:
        return jnp.where(lane >= LANES // 2, swapped, zero)
    if amount == -NQ:
        return jnp.where(lane < LANES // 2, swapped, zero)
    near = pltpu.roll(tile, amount % NQ, 0)
    far = pltpu.roll(swapped, amount % NQ, 0)
    if amount > 0:
        return jnp.where(sub >= amount, near, jnp.where(lane >= LANES // 2, far, zero))
    return jnp.where(sub < NQ + amount, near, jnp.where(lane < LANES // 2, far, zero))


def product(left, right):
    return [
        [sum_of([left[v][x] * right[x][w] for x in range(NV)]) for w in range(NV)]
        for v in range(NV)
    ]


def sum_of(terms):
    while len(terms) > 1:
        terms = [
            terms[i] + terms[i + 1] if i + 1 < len(terms) else terms[i]
            for i in range(0, len(terms), 2)
        ]
    return terms[0]


def applied(coef_ref, index, vector):
    return [
        sum_of([coef_ref[(v * NV + w, *index)] * vector[w] for w in range(NV)]) for v in range(NV)
    ]


def tables_kernel(
    factor_ref, lower_ref, upper_ref, a_ref, b_ref, phi_ref, omega_ref, up_ref, down_ref
):
    def load(ref, t):
        return [[ref[v * NV + w, t] for w in range(NV)] for v in range(NV)]

    def keep(ref, t, value):
        for v in range(NV):
            for w in range(NV):
                ref[v * NV + w, t] = value[v][w]

    lower = [[-lower_ref[v, w] for w in range(NV)] for v in range(NV)]
    upper = [[-upper_ref[v, w] for w in range(NV)] for v in range(NV)]

    def couple(t, carry):
        factor = load(factor_ref, t)
        keep(a_ref, t, product(factor, lower))
        keep(b_ref, t, product(factor, upper))
        return carry

    lax.fori_loop(0, NS, couple, 0)
    keep(phi_ref, 0, load(a_ref, 0))
    keep(omega_ref, NS - 1, load(b_ref, NS - 1))

    def extend(t, carry):
        keep(phi_ref, t, product(load(a_ref, t), load(phi_ref, t - 1)))
        back = NS - 1 - t
        keep(omega_ref, back, product(load(b_ref, back), load(omega_ref, back + 1)))
        return carry

    lax.fori_loop(1, NS, extend, 0)
    for ref, first, sign in ((up_ref, load(phi_ref, NS - 1), 1), (down_ref, load(omega_ref, 0), -1)):
        level = first
        for step in range(LEVELS):
            keep(ref, step, level)
            if step + 1 < LEVELS:
                moved = [[shift_chunks(e, sign * 2**step) for e in row] for row in level]
                level = product(level, moved)


def time_kernel(spectral_ref, state_ref, timed_ref):
    count = spectral_ref.shape[0]
    rows = state_ref.shape[0] // count
    stacked = jnp.concatenate(
        [state_ref[pl.ds(row, count, stride=rows), :] for row in range(rows)], axis=1
    )
    result = jnp.dot(
        spectral_ref[...],
        stacked,
        precision=lax.Precision.HIGHEST,
        preferred_element_type=jnp.float32,
    )
    for row in range(rows):
        timed_ref[pl.ds(row, count, stride=rows), :] = result[:, row * LANES : (row + 1) * LANES]


def to_lines(select, value):
    parts = []
    rest = value
    for part in range(3):
        head = rest.astype(jnp.bfloat16)
        parts.append(head)
        if part < 2:
            rest = rest - head.astype(jnp.float32)
    total = None
    for head in parts:
        blank = jnp.zeros_like(head[0])
        blocks = []
        for v in range(NV):
            blocks.append(jnp.concatenate([head[v], blank], axis=1))
            blocks.append(jnp.concatenate([blank, head[v]], axis=1))
        moved = lax.dot_general(
            select,
            jnp.concatenate(blocks, axis=0),
            (((1,), (1,)), ((), ())),
            preferred_element_type=jnp.float32,
        )
        total = moved if total is None else total + moved
    return total


def local_kernel(
    state_ref, forcing_ref, low_ref, high_ref, select_ref, axial_ref, radial_ref, local_ref
):
    stations = state_ref.shape[1]
    row = lax.broadcasted_iota(jnp.int32, (stations, LANES), 0)
    state = [state_ref[v] for v in range(NV)]
    ahead = [
        jnp.where(row == stations - 1, high_ref[v : v + 1], pltpu.roll(state[v], stations - 1, 0))
        for v in range(NV)
    ]
    behind = [
        jnp.where(row == 0, low_ref[v : v + 1], pltpu.roll(state[v], 1, 0)) for v in range(NV)
    ]
    slope = [0.5 * (ahead[v] - behind[v]) for v in range(NV)]
    direct = [
        sum_of([axial_ref[v, w] * slope[w] for w in range(NV)])
        - damping * (ahead[v] + behind[v] - 4.0 * state[v])
        - forcing_ref[v]
        for v in range(NV)
    ]
    select = select_ref[...]
    lines = to_lines(select, jnp.stack(state))
    moved = to_lines(select, jnp.stack(direct))

    def tile(array, v, t):
        return array[t * NQ : (t + 1) * NQ, v * LANES : (v + 1) * LANES]

    for t in range(NS):
        outer = [
            tile(lines, v, t + 1) if t + 1 < NS else shift_chunks(tile(lines, v, 0), -1)
            for v in range(NV)
        ]
        inner = [
            tile(lines, v, t - 1) if t > 0 else shift_chunks(tile(lines, v, NS - 1), 1)
            for v in range(NV)
        ]
        slope = [0.5 * (outer[v] - inner[v]) for v in range(NV)]
        for v in range(NV):
            local_ref[v, t] = (
                sum_of([radial_ref[v, w] * slope[w] for w in range(NV)])
                - damping * (outer[v] + inner[v])
                + tile(moved, v, t)
            )


def from_lines(lines_ref, out_ref):
    lane = lax.broadcasted_iota(jnp.int32, (LANES // 2, LANES), 1)
    half = LANES // 2
    for pair in range(NV // 2):
        rows = [
            lines_ref[2 * pair + p, pl.ds(sub, NS, stride=NQ), :]
            for p in range(2)
            for sub in range(NQ)
        ]
        turned = jnp.concatenate(rows, axis=0).T
        top, bottom = turned[:half], turned[half:]
        out_ref[2 * pair] = jnp.where(lane < half, top, pltpu.roll(bottom, half, 1))
        out_ref[2 * pair + 1] = jnp.where(lane < half, pltpu.roll(top, half, 1), bottom)


def solve_kernel(
    timed_ref,
    local_ref,
    select_ref,
    factor_ref,
    a_ref,
    b_ref,
    phi_ref,
    omega_ref,
    up_ref,
    down_ref,
    residual_ref,
    correction_ref,
    lines_ref,
):
    moved = to_lines(select_ref[...], timed_ref[...])
    sweep = []
    for t in range(NS):
        residual = []
        for v in range(NV):
            value = (
                moved[t * NQ : (t + 1) * NQ, v * LANES : (v + 1) * LANES] + local_ref[v, t]
            )
            lines_ref[v, t * NQ : (t + 1) * NQ] = value
            residual.append(value)
        value = applied(factor_ref, (t,), residual)
        if t > 0:
            before = applied(a_ref, (t,), sweep[t - 1])
            value = [x + y for x, y in zip(value, before)]
        sweep.append(value)
    from_lines(lines_ref, residual_ref)

    carry = sweep[NS - 1]
    for step in range(LEVELS):
        more = applied(up_ref, (step,), [shift_chunks(x, 2**step) for x in carry])
        carry = [x + y for x, y in zip(carry, more)]
    carry = [shift_chunks(x, 1) for x in carry]
    back = [None] * NS
    for t in reversed(range(NS)):
        more = applied(phi_ref, (t,), carry)
        value = [x + y for x, y in zip(sweep[t], more)]
        if t + 1 < NS:
            more = applied(b_ref, (t,), back[t + 1])
            value = [x + y for x, y in zip(value, more)]
        back[t] = value
    carry = back[0]
    for step in range(LEVELS):
        more = applied(down_ref, (step,), [shift_chunks(x, -(2**step)) for x in carry])
        carry = [x + y for x, y in zip(carry, more)]
    carry = [shift_chunks(x, -1) for x in carry]
    for t in range(NS):
        more = applied(omega_ref, (t,), carry)
        for v in range(NV):
            lines_ref[v, t * NQ : (t + 1) * NQ] = back[t][v] + more[v]
    from_lines(lines_ref, correction_ref)


VMEM = pl.BlockSpec(memory_space=pltpu.VMEM)
SMEM = pl.BlockSpec(memory_space=pltpu.SMEM)
MIB = 2**20


def f32(*shape):
    return jax.ShapeDtypeStruct(shape, jnp.float32)


def call(body, outs, specs, operands, limit, flops, scratch=()):
    moved = sum(x.size * x.dtype.itemsize for x in operands)
    moved += sum(4 * o.size for o in outs)
    return pl.pallas_call(
        body,
        out_shape=outs,
        in_specs=specs,
        out_specs=[VMEM] * len(outs),
        scratch_shapes=list(scratch),
        compiler_params=pltpu.CompilerParams(vmem_limit_bytes=limit * MIB),
        cost_estimate=pl.CostEstimate(flops=flops, bytes_accessed=moved, transcendentals=0),
    )(*operands)


def shards(
    flow_state,
    forcing,
    pivot_table,
    block_offset,
    line_perm,
    axial_jac,
    radial_jac,
    lower_block,
    upper_block,
):
    hp = lax.Precision.HIGHEST
    state = flow_state[0]
    count = lax.axis_size("inst")
    variables, stations, radial = state.shape
    share = variables * stations // count

    gathered = lax.all_to_all(
        state.reshape(count, share // 4, 4, radial), "inst", 0, 0, tiled=True
    )
    (timed,) = call(
        time_kernel,
        [f32(count * share, radial)],
        [VMEM, VMEM],
        [spectral_matrix(count), gathered.reshape(count * share, radial)],
        4,
        2 * count * count * share * radial,
    )
    timed = lax.all_to_all(
        timed.reshape(count, share // 4, 4, radial), "inst", 0, 0, tiled=True
    ).reshape(variables, stations, radial)

    chips = lax.axis_size("space")
    up = [(i, i + 1) for i in range(chips - 1)]
    low = lax.ppermute(state[:, stations - 1], "space", up)
    high = lax.ppermute(state[:, 0], "space", [(target, source) for source, target in up])

    table = pivot_table.reshape(KB, NV * NV, NH, NQ, NS).transpose(1, 4, 3, 2, 0)
    chosen = (block_offset[None] == lax.broadcasted_iota(jnp.int32, (KB, stations), 0)).astype(
        jnp.float32
    )
    blank = jnp.zeros_like(chosen)
    chosen = jnp.concatenate(
        [jnp.concatenate([chosen, blank], 1), jnp.concatenate([blank, chosen], 1)], 0
    )
    factor = jnp.dot(table.reshape(-1, NH * KB), chosen, precision=hp)
    factor = factor.reshape(NV * NV, NS, NQ, LANES)
    order = line_perm.reshape(NH, NQ, NS).transpose(2, 1, 0).reshape(NS * NQ, NH, 1)
    select = order == lax.broadcasted_iota(jnp.int32, (NS * NQ, NH, radial), 2)
    select = select.astype(jnp.bfloat16).reshape(NS * NQ, NH * radial)

    coef = f32(NV * NV, NS, NQ, LANES)
    level = f32(NV * NV, LEVELS, NQ, LANES)
    tables = call(
        tables_kernel,
        [coef, coef, coef, coef, level, level],
        [VMEM, SMEM, SMEM],
        [factor, lower_block, upper_block],
        12,
        36 * 6 * 2 * 1024 * 40,
    )
    (local,) = call(
        local_kernel,
        [f32(NV, NS, NQ, LANES)],
        [VMEM, VMEM, VMEM, VMEM, VMEM, SMEM, SMEM],
        [state, forcing[0], low, high, select, axial_jac, radial_jac],
        8,
        2 * 768 * 64 * 256 * 6,
    )
    residual, correction = call(
        solve_kernel,
        [f32(variables, stations, radial)] * 2,
        [VMEM] * 10,
        [timed, local, select, factor, *tables],
        16,
        36 * 2 * 1024 * 50,
        [pltpu.VMEM((NV, NS * NQ, LANES), jnp.float32)],
    )
    return residual[None], correction[None]


def solution(mesh):
    return jax.shard_map(
        shards,
        mesh=mesh,
        in_specs=(
            P("inst", None, "space", None),
            P("inst", None, "space", None),
            P(),
            P("space"),
            P(),
            P(),
            P(),
            P(),
            P(),
        ),
        out_specs=(P("inst", None, "space", None), P("inst", None, "space", None)),
        check_vma=False,
    )
```

```python
import jax
import jax.numpy as jnp
from jax import lax
from jax.experimental import pallas as pl
from jax.experimental.pallas import tpu as pltpu
from jax.sharding import PartitionSpec as P

frequency = 0.5
viscosity = 0.01
damping = 0.25

NV = 6
NQ = 8
NS = 8
NH = 2
KB = 8
LANES = 128
LEVELS = 4


def spectral_matrix(count):
    row_index = lax.broadcasted_iota(jnp.int32, (count, count), 0)
    col_index = lax.broadcasted_iota(jnp.int32, (count, count), 1)
    distance = row_index - col_index
    parity = (1 - 2 * jnp.mod(distance, 2)).astype(jnp.float32)
    phase_angle = jnp.pi * distance.astype(jnp.float32) / count
    diagonal_mask = distance == 0
    sine_value = jnp.where(diagonal_mask, 1.0, jnp.sin(phase_angle))
    first_order = jnp.where(diagonal_mask, 0.0, 0.5 * parity * jnp.cos(phase_angle) / sine_value)
    second_order = jnp.where(
        diagonal_mask, -(count * count + 2) / 12.0, -0.5 * parity / (sine_value * sine_value)
    )
    return frequency * first_order - viscosity * second_order


def shift_chunks(tile, amount):
    sub = lax.broadcasted_iota(jnp.int32, tile.shape, 0)
    lane = lax.broadcasted_iota(jnp.int32, tile.shape, 1)
    zero = jnp.zeros_like(tile)
    swapped = pltpu.roll(tile, LANES // 2, 1)
    if amount == NQ:
        return jnp.where(lane >= LANES // 2, swapped, zero)
    if amount == -NQ:
        return jnp.where(lane < LANES // 2, swapped, zero)
    near = pltpu.roll(tile, amount % NQ, 0)
    far = pltpu.roll(swapped, amount % NQ, 0)
    if amount > 0:
        return jnp.where(sub >= amount, near, jnp.where(lane >= LANES // 2, far, zero))
    return jnp.where(sub < NQ + amount, near, jnp.where(lane < LANES // 2, far, zero))


def product(left, right):
    return [
        [sum_of([left[v][x] * right[x][w] for x in range(NV)]) for w in range(NV)]
        for v in range(NV)
    ]


def sum_of(terms):
    while len(terms) > 1:
        terms = [
            terms[i] + terms[i + 1] if i + 1 < len(terms) else terms[i]
            for i in range(0, len(terms), 2)
        ]
    return terms[0]


def applied(coef_ref, index, vector):
    return [
        sum_of([coef_ref[(v * NV + w, *index)] * vector[w] for w in range(NV)]) for v in range(NV)
    ]


def split(value):
    high = value.astype(jnp.bfloat16)
    rest = value - high.astype(jnp.float32)
    middle = rest.astype(jnp.bfloat16)
    return high, middle, (rest - middle.astype(jnp.float32)).astype(jnp.bfloat16)


def picked(select, value):
    dims = (((1,), (1,)), ((), ()))
    parts = [
        lax.dot_general(select, part, dims, preferred_element_type=jnp.float32)
        for part in split(value)
    ]
    return parts[0] + parts[1] + parts[2]


def doubled(planes):
    blank = jnp.zeros_like(planes[0])
    blocks = []
    for plane in planes:
        blocks.append(jnp.concatenate([plane, blank], axis=1))
        blocks.append(jnp.concatenate([blank, plane], axis=1))
    return jnp.concatenate(blocks, axis=0)


def fetch(pairs, sems):
    copies = [pltpu.make_async_copy(x, y, sems.at[i]) for i, (x, y) in enumerate(pairs)]
    for copy in copies:
        copy.start()
    return copies


def prepare_kernel(*refs):
    table_hbm, offset_hbm, order_hbm, state_hbm, forcing_hbm = refs[:5]
    lower_ref, upper_ref, axial_ref, radial_ref = refs[5:9]
    factor_ref, a_ref, up_ref, local_ref, select_ref, b_out, down_out = refs[9:16]
    table_ref, offset_ref, order_ref, state_ref, forcing_ref = refs[16:21]
    b_ref, down_ref, turned_ref, sems, b_sem, down_sem = refs[21:]
    copies = fetch(
        [
            (order_hbm, order_ref),
            (offset_hbm, offset_ref),
            (table_hbm, table_ref),
            (state_hbm, state_ref),
            (forcing_hbm, forcing_ref),
        ],
        sems,
    )
    for copy in copies[:3]:
        copy.wait()
    slot = lax.broadcasted_iota(jnp.int32, (LANES, LANES), 0)
    turned_ref[...] = (slot == order_ref[...]).astype(jnp.float32).T
    halves = [
        jnp.concatenate(
            [turned_ref[pl.ds(half * NS * NQ + t, NQ, stride=NS), :] for t in range(NS)], axis=0
        )
        for half in range(NH)
    ]
    select = jnp.concatenate(halves, axis=1).astype(jnp.bfloat16)
    select_ref[...] = select

    tables = [[table_ref[v * NV + w] for w in range(NV)] for v in range(NV)]
    lower = [[-lower_ref[v, w] for w in range(NV)] for v in range(NV)]
    upper = [[-upper_ref[v, w] for w in range(NV)] for v in range(NV)]
    row = lax.broadcasted_iota(jnp.int32, (NS * NQ, NH * LANES), 0)
    column = lax.broadcasted_iota(jnp.int32, (NS * NQ, NH * LANES), 1)
    place = (row % NQ) * NS + row // NQ
    place = jnp.where(column < LANES, place, place + LANES + NS * NQ)
    lines = (column == place).astype(jnp.bfloat16)
    lane = lax.broadcasted_iota(jnp.int32, (NS * NQ, LANES), 1)
    offset = jnp.concatenate([offset_ref[...], offset_ref[...]], axis=1)
    index = jnp.where(lane < LANES // 2, 0, KB) + offset
    group = LANES // (NH * KB)

    def spread(value, ref):
        planes = [e for line in value for e in line]
        padding = [jnp.zeros_like(planes[0])] * (-len(planes) % group)
        moved = picked(lines, doubled(planes + padding))
        for i in range(NV * NV):
            start = i // group * LANES
            source = moved[:, start : start + LANES]
            chosen = jnp.take_along_axis(source, index + (i % group) * NH * KB, axis=1)
            for t in range(NS):
                ref[i, t] = chosen[t * NQ : (t + 1) * NQ]

    def load(ref, t):
        return [[ref[v * NV + w, t] for w in range(NV)] for v in range(NV)]

    def keep(ref, t, value):
        for v in range(NV):
            for w in range(NV):
                ref[v * NV + w, t] = value[v][w]

    spread(product(tables, upper), b_ref)
    spread(product(tables, lower), a_ref)
    spread(tables, factor_ref)
    stores = fetch([(b_ref, b_out)], b_sem)
    keep(up_ref, 0, load(a_ref, 0))
    keep(down_ref, 0, load(b_ref, NS - 1))

    def extend(t, carry):
        keep(up_ref, 0, product(load(a_ref, t), load(up_ref, 0)))
        keep(down_ref, 0, product(load(b_ref, NS - 1 - t), load(down_ref, 0)))
        return carry

    lax.fori_loop(1, NS, extend, 0)
    for ref, sign in ((up_ref, 1), (down_ref, -1)):
        for step in range(1, LEVELS):
            level = load(ref, step - 1)
            moved = [[shift_chunks(e, sign * 2 ** (step - 1)) for e in line] for line in level]
            keep(ref, step, product(level, moved))

    stores += fetch([(down_ref, down_out)], down_sem)
    for copy in copies[3:]:
        copy.wait()
    stations = state_ref.shape[1]
    row = lax.broadcasted_iota(jnp.int32, (stations, LANES), 0)
    state = [state_ref[v] for v in range(NV)]
    ahead = [
        jnp.where(row == stations - 1, 0.0, pltpu.roll(state[v], stations - 1, 0))
        for v in range(NV)
    ]
    behind = [jnp.where(row == 0, 0.0, pltpu.roll(state[v], 1, 0)) for v in range(NV)]
    slope = [0.5 * (ahead[v] - behind[v]) for v in range(NV)]
    direct = [
        sum_of([axial_ref[v, w] * slope[w] for w in range(NV)])
        - damping * (ahead[v] + behind[v] - 4.0 * state[v])
        - forcing_ref[v]
        for v in range(NV)
    ]
    lines = picked(select, doubled(state))
    moved = picked(select, doubled(direct))

    def tile(array, v, t):
        return array[t * NQ : (t + 1) * NQ, v * LANES : (v + 1) * LANES]

    for t in range(NS):
        outer = [
            tile(lines, v, t + 1) if t + 1 < NS else shift_chunks(tile(lines, v, 0), -1)
            for v in range(NV)
        ]
        inner = [
            tile(lines, v, t - 1) if t > 0 else shift_chunks(tile(lines, v, NS - 1), 1)
            for v in range(NV)
        ]
        slope = [0.5 * (outer[v] - inner[v]) for v in range(NV)]
        for v in range(NV):
            local_ref[v, t] = (
                sum_of([radial_ref[v, w] * slope[w] for w in range(NV)])
                - damping * (outer[v] + inner[v])
                + tile(moved, v, t)
            )
    for copy in stores:
        copy.wait()


def time_kernel(spectral_ref, state_ref, timed_hbm, timed_ref, sem):
    count = spectral_ref.shape[0]
    rows = state_ref.shape[0] // count
    high, middle, low = split(spectral_ref[...])
    weight = jnp.concatenate([high, high, middle, high, low, middle], axis=1)
    stacked = jnp.concatenate(
        [state_ref[pl.ds(row, count, stride=rows), :] for row in range(rows)], axis=1
    )
    high, middle, low = split(stacked)
    result = jnp.dot(
        weight,
        jnp.concatenate([high, middle, high, low, high, middle], axis=0),
        preferred_element_type=jnp.float32,
    )
    for row in range(rows):
        timed_ref[pl.ds(row, count, stride=rows), :] = result[:, row * LANES : (row + 1) * LANES]
    copy = pltpu.make_async_copy(timed_ref, timed_hbm, sem)
    copy.start()
    copy.wait()


def from_lines(lines_ref, out_ref, out_hbm, sems):
    lane = lax.broadcasted_iota(jnp.int32, (LANES // 2, LANES), 1)
    half = LANES // 2
    copies = []
    for pair in range(NV // 2):
        rows = [
            lines_ref[2 * pair + p, pl.ds(sub, NS, stride=NQ), :]
            for p in range(2)
            for sub in range(NQ)
        ]
        turned = jnp.concatenate(rows, axis=0).T
        top, bottom = turned[:half], turned[half:]
        out_ref[2 * pair] = jnp.where(lane < half, top, pltpu.roll(bottom, half, 1))
        out_ref[2 * pair + 1] = jnp.where(lane < half, pltpu.roll(top, half, 1), bottom)
        both = pl.ds(2 * pair, 2)
        copies.append(pltpu.make_async_copy(out_ref.at[both], out_hbm.at[both], sems.at[pair]))
        copies[-1].start()
    return copies


def solve_kernel(*refs):
    timed_ref, select_ref, local_ref, factor_ref, a_ref, up_ref, swap_ref, other_ref = refs[:8]
    b_hbm, down_hbm, parity_ref, axial_ref, residual_hbm, correction_hbm = refs[8:14]
    joined_ref, b_ref, down_ref, residual_ref, correction_ref, lines_ref = refs[14:20]
    sems, residual_sems, correction_sems = refs[20:]
    loads = fetch([(b_hbm, b_ref), (down_hbm, down_ref)], sems)
    even = parity_ref[0] == 0
    high = [jnp.where(even, swap_ref[v, 0, :1], other_ref[v, 0, :1]) for v in range(NV)]
    low = [
        jnp.where(even, other_ref[v, 1, NQ - 1 :], swap_ref[v, 1, NQ - 1 :])
        for v in range(NV)
    ]
    row = lax.broadcasted_iota(jnp.int32, (NQ, LANES), 0)
    stations = timed_ref.shape[1]
    for v in range(NV):
        before = sum_of([-0.5 * axial_ref[v, w] * low[w] for w in range(NV)]) - damping * low[v]
        after = sum_of([0.5 * axial_ref[v, w] * high[w] for w in range(NV)]) - damping * high[v]
        joined_ref[v, :NQ] = timed_ref[v, :NQ] + jnp.where(row == 0, before, 0.0)
        joined_ref[v, NQ : stations - NQ] = timed_ref[v, NQ : stations - NQ]
        joined_ref[v, stations - NQ :] = timed_ref[v, stations - NQ :] + jnp.where(
            row == NQ - 1, after, 0.0
        )
    moved = picked(select_ref[...], doubled([joined_ref[v] for v in range(NV)]))
    own = []
    ends = None
    for t in range(NS):
        residual = []
        for v in range(NV):
            value = (
                moved[t * NQ : (t + 1) * NQ, v * LANES : (v + 1) * LANES] + local_ref[v, t]
            )
            lines_ref[v, t * NQ : (t + 1) * NQ] = value
            residual.append(value)
        value = applied(factor_ref, (t,), residual)
        own.append(value)
        if t > 0:
            value = [x + y for x, y in zip(value, applied(a_ref, (t,), ends))]
        ends = value
    copies = from_lines(lines_ref, residual_ref, residual_hbm, residual_sems)

    for step in range(LEVELS):
        more = applied(up_ref, (step,), [shift_chunks(x, 2**step) for x in ends])
        ends = [x + y for x, y in zip(ends, more)]
    carry = [shift_chunks(x, 1) for x in ends]
    sweep = []
    for t in range(NS):
        carry = [x + y for x, y in zip(own[t], applied(a_ref, (t,), carry))]
        sweep.append(carry)
    for copy in loads:
        copy.wait()
    ends = sweep[NS - 1]
    for t in reversed(range(NS - 1)):
        ends = [x + y for x, y in zip(sweep[t], applied(b_ref, (t,), ends))]
    for step in range(LEVELS):
        more = applied(down_ref, (step,), [shift_chunks(x, -(2**step)) for x in ends])
        ends = [x + y for x, y in zip(ends, more)]
    carry = [shift_chunks(x, -1) for x in ends]
    for t in reversed(range(NS)):
        carry = [x + y for x, y in zip(sweep[t], applied(b_ref, (t,), carry))]
        for v in range(NV):
            lines_ref[v, t * NQ : (t + 1) * NQ] = carry[v]
    copies += from_lines(lines_ref, correction_ref, correction_hbm, correction_sems)
    for copy in copies:
        copy.wait()


SMEM = pl.BlockSpec(memory_space=pltpu.SMEM)
VMEM = pl.BlockSpec(memory_space=pltpu.VMEM)
MIB = 2**20
ANY = pl.BlockSpec(memory_space=pl.ANY)
PREP = 10**10


def f32(*shape):
    return jax.ShapeDtypeStruct(shape, jnp.float32)


def call(body, near, far, small, near_outs, far_outs, limit, flops, scratch):
    operands = [pltpu.with_memory_space_constraint(x, pltpu.VMEM) for x in near]
    operands += [pltpu.with_memory_space_constraint(x, pltpu.HBM) for x in far]
    outs = [pltpu.VMEM(x.shape, x.dtype) for x in near_outs]
    outs += [pltpu.HBM(x.shape, x.dtype) for x in far_outs]
    moved = sum(x.size * x.dtype.itemsize for x in [*near, *far, *near_outs, *far_outs])
    return pl.pallas_call(
        body,
        out_shape=outs,
        in_specs=[VMEM] * len(near) + [ANY] * len(far) + [SMEM] * len(small),
        out_specs=[VMEM] * len(near_outs) + [ANY] * len(far_outs),
        scratch_shapes=list(scratch),
        compiler_params=pltpu.CompilerParams(vmem_limit_bytes=limit * MIB),
        cost_estimate=pl.CostEstimate(flops=flops, bytes_accessed=moved, transcendentals=0),
    )(*operands, *small)


def shards(
    flow_state,
    forcing,
    pivot_table,
    block_offset,
    line_perm,
    axial_jac,
    radial_jac,
    lower_block,
    upper_block,
):
    state = flow_state[0]
    count = lax.axis_size("inst")
    variables, stations, radial = state.shape
    share = variables * stations // count

    gathered = lax.all_to_all(
        state.reshape(count, share // 4, 4, radial), "inst", 0, 0, tiled=True
    )

    edges = state.reshape(variables, stations // NQ, NQ, radial)
    edges = edges[:, :: stations // NQ - 1]
    chips = lax.axis_size("space")
    swap = lax.ppermute(edges, "space", [(i, i ^ 1) for i in range(chips)])
    other = lax.ppermute(edges, "space", [(i, ((i + 1) ^ 1) - 1) for i in range(1, chips - 1)])
    dma = pltpu.SemaphoreType.DMA

    (timed,) = call(
        time_kernel,
        [spectral_matrix(count), gathered.reshape(count * share, radial)],
        [],
        [],
        [],
        [f32(count * share, radial)],
        8,
        2 * count * count * share * radial,
        [pltpu.VMEM((count * share, radial), jnp.float32), dma],
    )
    timed, state = lax.optimization_barrier((timed, state))
    timed = lax.all_to_all(
        timed.reshape(count, share // 4, 4, radial), "inst", 0, 0, tiled=True
    ).reshape(variables, stations, radial)

    coef = f32(NV * NV, NS, NQ, LANES)
    level = f32(NV * NV, LEVELS, NQ, LANES)
    lines = f32(NV, NS, NQ, LANES)
    one_hot = jax.ShapeDtypeStruct((NS * NQ, NH * LANES), jnp.bfloat16)
    cells = f32(variables, stations, radial)

    def scratch(*shapes):
        return [pltpu.VMEM(x.shape, x.dtype) for x in shapes]

    inputs = [
        pivot_table.transpose(1, 2, 0, 3).reshape(NV * NV, KB, radial),
        block_offset.reshape(1, stations),
        line_perm.reshape(1, radial),
        state,
        forcing[0],
    ]
    factor, a_table, up_table, local, select, b_table, down_table = call(
        prepare_kernel,
        [],
        inputs,
        [lower_block, upper_block, axial_jac, radial_jac],
        [coef, coef, level, lines, one_hot],
        [coef, level],
        16,
        PREP,
        scratch(*inputs, coef, level, f32(LANES, LANES)) + [dma((5,)), dma((1,)), dma((1,))],
    )
    parity = (lax.axis_index("space") % 2).astype(jnp.int32).reshape(1)
    residual, correction = call(
        solve_kernel,
        [timed, select, local, factor, a_table, up_table, swap, other],
        [b_table, down_table],
        [parity, axial_jac],
        [],
        [cells, cells],
        16,
        36 * 2 * 1024 * 50,
        scratch(cells, coef, level, cells, cells)
        + [
            pltpu.VMEM((NV, NS * NQ, LANES), jnp.float32),
            dma((2,)),
            dma((NV // 2,)),
            dma((NV // 2,)),
        ],
    )
    return residual[None], correction[None]


def solution(mesh):
    return jax.shard_map(
        shards,
        mesh=mesh,
        in_specs=(
            P("inst", None, "space", None),
            P("inst", None, "space", None),
            P(),
            P("space"),
            P(),
            P(),
            P(),
            P(),
            P(),
        ),
        out_specs=(P("inst", None, "space", None), P("inst", None, "space", None)),
        check_vma=False,
    )
```

```python
import jax
import jax.numpy as jnp
from jax import lax
from jax.experimental import pallas as pl
from jax.experimental.pallas import tpu as pltpu
from jax.sharding import PartitionSpec as P

frequency = 0.5
viscosity = 0.01
damping = 0.25

NV = 6
NQ = 8
NS = 8
NH = 2
KB = 8
LANES = 128
LEVELS = 4


def spectral_matrix(count):
    row_index = lax.broadcasted_iota(jnp.int32, (count, count), 0)
    col_index = lax.broadcasted_iota(jnp.int32, (count, count), 1)
    distance = row_index - col_index
    parity = (1 - 2 * jnp.mod(distance, 2)).astype(jnp.float32)
    phase_angle = jnp.pi * distance.astype(jnp.float32) / count
    diagonal_mask = distance == 0
    sine_value = jnp.where(diagonal_mask, 1.0, jnp.sin(phase_angle))
    first_order = jnp.where(diagonal_mask, 0.0, 0.5 * parity * jnp.cos(phase_angle) / sine_value)
    second_order = jnp.where(
        diagonal_mask, -(count * count + 2) / 12.0, -0.5 * parity / (sine_value * sine_value)
    )
    return frequency * first_order - viscosity * second_order


def shift_chunks(tile, amount):
    sub = lax.broadcasted_iota(jnp.int32, tile.shape, 0)
    lane = lax.broadcasted_iota(jnp.int32, tile.shape, 1)
    zero = jnp.zeros_like(tile)
    swapped = pltpu.roll(tile, LANES // 2, 1)
    if amount == NQ:
        return jnp.where(lane >= LANES // 2, swapped, zero)
    if amount == -NQ:
        return jnp.where(lane < LANES // 2, swapped, zero)
    near = pltpu.roll(tile, amount % NQ, 0)
    far = pltpu.roll(swapped, amount % NQ, 0)
    if amount > 0:
        return jnp.where(sub >= amount, near, jnp.where(lane >= LANES // 2, far, zero))
    return jnp.where(sub < NQ + amount, near, jnp.where(lane < LANES // 2, far, zero))


def product(left, right):
    return [
        [sum_of([left[v][x] * right[x][w] for x in range(NV)]) for w in range(NV)]
        for v in range(NV)
    ]


def sum_of(terms):
    while len(terms) > 1:
        terms = [
            terms[i] + terms[i + 1] if i + 1 < len(terms) else terms[i]
            for i in range(0, len(terms), 2)
        ]
    return terms[0]


def applied(coef_ref, index, vector):
    return [
        sum_of([coef_ref[(v * NV + w, *index)] * vector[w] for w in range(NV)]) for v in range(NV)
    ]


def split(value):
    high = value.astype(jnp.bfloat16)
    rest = value - high.astype(jnp.float32)
    middle = rest.astype(jnp.bfloat16)
    return high, middle, (rest - middle.astype(jnp.float32)).astype(jnp.bfloat16)


def picked(select, value):
    dims = (((1,), (1,)), ((), ()))
    parts = [
        lax.dot_general(select, part, dims, preferred_element_type=jnp.float32)
        for part in split(value)
    ]
    return parts[0] + parts[1] + parts[2]


def doubled(planes):
    blank = jnp.zeros_like(planes[0])
    blocks = []
    for plane in planes:
        blocks.append(jnp.concatenate([plane, blank], axis=1))
        blocks.append(jnp.concatenate([blank, plane], axis=1))
    return jnp.concatenate(blocks, axis=0)


def fetch(pairs, sems):
    copies = [pltpu.make_async_copy(x, y, sems.at[i]) for i, (x, y) in enumerate(pairs)]
    for copy in copies:
        copy.start()
    return copies


def prepare_kernel(*refs):
    table_hbm, offset_hbm, order_hbm, state_hbm, forcing_hbm = refs[:5]
    lower_ref, upper_ref, axial_ref, radial_ref = refs[5:9]
    factor_ref, a_ref, up_ref, local_ref, select_ref, b_out, down_out = refs[9:16]
    table_ref, offset_ref, order_ref, state_ref, forcing_ref = refs[16:21]
    b_ref, down_ref, turned_ref, sems, b_sem, down_sem = refs[21:]
    copies = fetch(
        [
            (order_hbm, order_ref),
            (offset_hbm, offset_ref),
            (table_hbm, table_ref),
            (state_hbm, state_ref),
            (forcing_hbm, forcing_ref),
        ],
        sems,
    )
    for copy in copies[:3]:
        copy.wait()
    slot = lax.broadcasted_iota(jnp.int32, (LANES, LANES), 0)
    turned_ref[...] = (slot == order_ref[...]).astype(jnp.float32).T
    halves = [
        jnp.concatenate(
            [turned_ref[pl.ds(half * NS * NQ + t, NQ, stride=NS), :] for t in range(NS)], axis=0
        )
        for half in range(NH)
    ]
    select = jnp.concatenate(halves, axis=1).astype(jnp.bfloat16)
    select_ref[...] = select

    tables = [[table_ref[v * NV + w] for w in range(NV)] for v in range(NV)]
    lower = [[-lower_ref[v, w] for w in range(NV)] for v in range(NV)]
    upper = [[-upper_ref[v, w] for w in range(NV)] for v in range(NV)]
    row = lax.broadcasted_iota(jnp.int32, (NS * NQ, NH * LANES), 0)
    column = lax.broadcasted_iota(jnp.int32, (NS * NQ, NH * LANES), 1)
    place = (row % NQ) * NS + row // NQ
    place = jnp.where(column < LANES, place, place + LANES + NS * NQ)
    lines = (column == place).astype(jnp.bfloat16)
    lane = lax.broadcasted_iota(jnp.int32, (NS * NQ, LANES), 1)
    offset = jnp.concatenate([offset_ref[...], offset_ref[...]], axis=1)
    index = jnp.where(lane < LANES // 2, 0, KB) + offset
    group = LANES // (NH * KB)

    def spread(value, ref):
        planes = [e for line in value for e in line]
        padding = [jnp.zeros_like(planes[0])] * (-len(planes) % group)
        moved = picked(lines, doubled(planes + padding))
        for i in range(NV * NV):
            start = i // group * LANES
            source = moved[:, start : start + LANES]
            chosen = jnp.take_along_axis(source, index + (i % group) * NH * KB, axis=1)
            for t in range(NS):
                ref[i, t] = chosen[t * NQ : (t + 1) * NQ]

    def load(ref, t):
        return [[ref[v * NV + w, t] for w in range(NV)] for v in range(NV)]

    def keep(ref, t, value):
        for v in range(NV):
            for w in range(NV):
                ref[v * NV + w, t] = value[v][w]

    spread(product(tables, upper), b_ref)
    spread(product(tables, lower), a_ref)
    spread(tables, factor_ref)
    stores = fetch([(b_ref, b_out)], b_sem)
    keep(up_ref, 0, load(a_ref, 0))
    keep(down_ref, 0, load(b_ref, NS - 1))

    def extend(t, carry):
        keep(up_ref, 0, product(load(a_ref, t), load(up_ref, 0)))
        keep(down_ref, 0, product(load(b_ref, NS - 1 - t), load(down_ref, 0)))
        return carry

    lax.fori_loop(1, NS, extend, 0)
    for ref, sign in ((up_ref, 1), (down_ref, -1)):
        for step in range(1, LEVELS):
            level = load(ref, step - 1)
            moved = [[shift_chunks(e, sign * 2 ** (step - 1)) for e in line] for line in level]
            keep(ref, step, product(level, moved))

    stores += fetch([(down_ref, down_out)], down_sem)
    for copy in copies[3:]:
        copy.wait()
    stations = state_ref.shape[1]
    row = lax.broadcasted_iota(jnp.int32, (stations, LANES), 0)
    state = [state_ref[v] for v in range(NV)]
    ahead = [
        jnp.where(row == stations - 1, 0.0, pltpu.roll(state[v], stations - 1, 0))
        for v in range(NV)
    ]
    behind = [jnp.where(row == 0, 0.0, pltpu.roll(state[v], 1, 0)) for v in range(NV)]
    slope = [0.5 * (ahead[v] - behind[v]) for v in range(NV)]
    direct = [
        sum_of([axial_ref[v, w] * slope[w] for w in range(NV)])
        - damping * (ahead[v] + behind[v] - 4.0 * state[v])
        - forcing_ref[v]
        for v in range(NV)
    ]
    lines = picked(select, doubled(state))
    moved = picked(select, doubled(direct))

    def tile(array, v, t):
        return array[t * NQ : (t + 1) * NQ, v * LANES : (v + 1) * LANES]

    for t in range(NS):
        outer = [
            tile(lines, v, t + 1) if t + 1 < NS else shift_chunks(tile(lines, v, 0), -1)
            for v in range(NV)
        ]
        inner = [
            tile(lines, v, t - 1) if t > 0 else shift_chunks(tile(lines, v, NS - 1), 1)
            for v in range(NV)
        ]
        slope = [0.5 * (outer[v] - inner[v]) for v in range(NV)]
        for v in range(NV):
            local_ref[v, t] = (
                sum_of([radial_ref[v, w] * slope[w] for w in range(NV)])
                - damping * (outer[v] + inner[v])
                + tile(moved, v, t)
            )
    for copy in stores:
        copy.wait()


def time_kernel(spectral_ref, state_ref, timed_hbm, timed_ref, sem):
    count = spectral_ref.shape[0]
    rows = state_ref.shape[0] // count
    high, middle, low = split(spectral_ref[...])
    weight = jnp.concatenate([high, high, middle, high, low, middle], axis=1)
    stacked = jnp.concatenate(
        [state_ref[pl.ds(row, count, stride=rows), :] for row in range(rows)], axis=1
    )
    high, middle, low = split(stacked)
    result = jnp.dot(
        weight,
        jnp.concatenate([high, middle, high, low, high, middle], axis=0),
        preferred_element_type=jnp.float32,
    )
    for row in range(rows):
        timed_ref[pl.ds(row, count, stride=rows), :] = result[:, row * LANES : (row + 1) * LANES]
    copy = pltpu.make_async_copy(timed_ref, timed_hbm, sem)
    copy.start()
    copy.wait()


def from_lines(lines_ref, out_ref, out_hbm, sems):
    lane = lax.broadcasted_iota(jnp.int32, (LANES // 2, LANES), 1)
    half = LANES // 2
    copies = []
    for pair in range(NV // 2):
        rows = [
            lines_ref[2 * pair + p, pl.ds(sub, NS, stride=NQ), :]
            for p in range(2)
            for sub in range(NQ)
        ]
        turned = jnp.concatenate(rows, axis=0).T
        top, bottom = turned[:half], turned[half:]
        out_ref[2 * pair] = jnp.where(lane < half, top, pltpu.roll(bottom, half, 1))
        out_ref[2 * pair + 1] = jnp.where(lane < half, pltpu.roll(top, half, 1), bottom)
        both = pl.ds(2 * pair, 2)
        copies.append(pltpu.make_async_copy(out_ref.at[both], out_hbm.at[both], sems.at[pair]))
        copies[-1].start()
    return copies


def solve_kernel(*refs):
    timed_ref, select_ref, local_ref, factor_ref, a_ref, up_ref, swap_ref, other_ref = refs[:8]
    b_hbm, down_hbm, parity_ref, axial_ref, residual_hbm, correction_hbm = refs[8:14]
    joined_ref, b_ref, down_ref, residual_ref, correction_ref, lines_ref = refs[14:20]
    sems, residual_sems, correction_sems = refs[20:]
    loads = fetch([(b_hbm, b_ref), (down_hbm, down_ref)], sems)
    even = parity_ref[0] == 0
    high = [jnp.where(even, swap_ref[v, 0, :1], other_ref[v, 0, :1]) for v in range(NV)]
    low = [
        jnp.where(even, other_ref[v, 1, NQ - 1 :], swap_ref[v, 1, NQ - 1 :])
        for v in range(NV)
    ]
    row = lax.broadcasted_iota(jnp.int32, (NQ, LANES), 0)
    stations = timed_ref.shape[1]
    for v in range(NV):
        before = sum_of([-0.5 * axial_ref[v, w] * low[w] for w in range(NV)]) - damping * low[v]
        after = sum_of([0.5 * axial_ref[v, w] * high[w] for w in range(NV)]) - damping * high[v]
        joined_ref[v, :NQ] = timed_ref[v, :NQ] + jnp.where(row == 0, before, 0.0)
        joined_ref[v, NQ : stations - NQ] = timed_ref[v, NQ : stations - NQ]
        joined_ref[v, stations - NQ :] = timed_ref[v, stations - NQ :] + jnp.where(
            row == NQ - 1, after, 0.0
        )
    moved = picked(select_ref[...], doubled([joined_ref[v] for v in range(NV)]))
    own = []
    ends = None
    for t in range(NS):
        residual = []
        for v in range(NV):
            value = (
                moved[t * NQ : (t + 1) * NQ, v * LANES : (v + 1) * LANES] + local_ref[v, t]
            )
            lines_ref[v, t * NQ : (t + 1) * NQ] = value
            residual.append(value)
        value = applied(factor_ref, (t,), residual)
        own.append(value)
        if t > 0:
            value = [x + y for x, y in zip(value, applied(a_ref, (t,), ends))]
        ends = value
    copies = from_lines(lines_ref, residual_ref, residual_hbm, residual_sems)

    for step in range(LEVELS):
        more = applied(up_ref, (step,), [shift_chunks(x, 2**step) for x in ends])
        ends = [x + y for x, y in zip(ends, more)]
    carry = [shift_chunks(x, 1) for x in ends]
    sweep = []
    for t in range(NS):
        carry = [x + y for x, y in zip(own[t], applied(a_ref, (t,), carry))]
        sweep.append(carry)
    for copy in loads:
        copy.wait()
    ends = sweep[NS - 1]
    for t in reversed(range(NS - 1)):
        ends = [x + y for x, y in zip(sweep[t], applied(b_ref, (t,), ends))]
    for step in range(LEVELS):
        more = applied(down_ref, (step,), [shift_chunks(x, -(2**step)) for x in ends])
        ends = [x + y for x, y in zip(ends, more)]
    carry = [shift_chunks(x, -1) for x in ends]
    for t in reversed(range(NS)):
        carry = [x + y for x, y in zip(sweep[t], applied(b_ref, (t,), carry))]
        for v in range(NV):
            lines_ref[v, t * NQ : (t + 1) * NQ] = carry[v]
    copies += from_lines(lines_ref, correction_ref, correction_hbm, correction_sems)
    for copy in copies:
        copy.wait()


SMEM = pl.BlockSpec(memory_space=pltpu.SMEM)
VMEM = pl.BlockSpec(memory_space=pltpu.VMEM)
MIB = 2**20
ANY = pl.BlockSpec(memory_space=pl.ANY)
PREP = 10**10


def f32(*shape):
    return jax.ShapeDtypeStruct(shape, jnp.float32)


def call(body, near, far, small, near_outs, far_outs, limit, flops, scratch):
    operands = [pltpu.with_memory_space_constraint(x, pltpu.VMEM) for x in near]
    operands += [pltpu.with_memory_space_constraint(x, pltpu.HBM) for x in far]
    outs = [pltpu.VMEM(x.shape, x.dtype) for x in near_outs]
    outs += [pltpu.HBM(x.shape, x.dtype) for x in far_outs]
    moved = sum(x.size * x.dtype.itemsize for x in [*near, *far, *near_outs, *far_outs])
    return pl.pallas_call(
        body,
        out_shape=outs,
        in_specs=[VMEM] * len(near) + [ANY] * len(far) + [SMEM] * len(small),
        out_specs=[VMEM] * len(near_outs) + [ANY] * len(far_outs),
        scratch_shapes=list(scratch),
        compiler_params=pltpu.CompilerParams(vmem_limit_bytes=limit * MIB),
        cost_estimate=pl.CostEstimate(flops=flops, bytes_accessed=moved, transcendentals=0),
    )(*operands, *small)


def shards(
    flow_state,
    forcing,
    pivot_table,
    block_offset,
    line_perm,
    axial_jac,
    radial_jac,
    lower_block,
    upper_block,
):
    state = flow_state[0]
    count = lax.axis_size("inst")
    variables, stations, radial = state.shape
    share = variables * stations // count

    gathered = lax.all_to_all(
        state.reshape(count, share // 4, 4, radial), "inst", 0, 0, tiled=True
    )

    edges = state.reshape(variables, stations // NQ, NQ, radial)
    edges = edges[:, :: stations // NQ - 1]
    chips = lax.axis_size("space")
    other = lax.ppermute(edges, "space", [(i, ((i + 1) ^ 1) - 1) for i in range(1, chips - 1)])
    dma = pltpu.SemaphoreType.DMA

    (timed,) = call(
        time_kernel,
        [spectral_matrix(count), gathered.reshape(count * share, radial)],
        [],
        [],
        [],
        [f32(count * share, radial)],
        8,
        2 * count * count * share * radial,
        [pltpu.VMEM((count * share, radial), jnp.float32), dma],
    )
    timed, state, edges = lax.optimization_barrier((timed, state, edges))
    swap = lax.ppermute(edges, "space", [(i, i ^ 1) for i in range(chips)])
    timed = lax.all_to_all(
        timed.reshape(count, share // 4, 4, radial), "inst", 0, 0, tiled=True
    ).reshape(variables, stations, radial)

    coef = f32(NV * NV, NS, NQ, LANES)
    level = f32(NV * NV, LEVELS, NQ, LANES)
    lines = f32(NV, NS, NQ, LANES)
    one_hot = jax.ShapeDtypeStruct((NS * NQ, NH * LANES), jnp.bfloat16)
    cells = f32(variables, stations, radial)

    def scratch(*shapes):
        return [pltpu.VMEM(x.shape, x.dtype) for x in shapes]

    inputs = [
        pivot_table.transpose(1, 2, 0, 3).reshape(NV * NV, KB, radial),
        block_offset.reshape(1, stations),
        line_perm.reshape(1, radial),
        state,
        forcing[0],
    ]
    factor, a_table, up_table, local, select, b_table, down_table = call(
        prepare_kernel,
        [],
        inputs,
        [lower_block, upper_block, axial_jac, radial_jac],
        [coef, coef, level, lines, one_hot],
        [coef, level],
        16,
        PREP,
        scratch(*inputs, coef, level, f32(LANES, LANES)) + [dma((5,)), dma((1,)), dma((1,))],
    )
    parity = (lax.axis_index("space") % 2).astype(jnp.int32).reshape(1)
    residual, correction = call(
        solve_kernel,
        [timed, select, local, factor, a_table, up_table, swap, other],
        [b_table, down_table],
        [parity, axial_jac],
        [],
        [cells, cells],
        16,
        36 * 2 * 1024 * 50,
        scratch(cells, coef, level, cells, cells)
        + [
            pltpu.VMEM((NV, NS * NQ, LANES), jnp.float32),
            dma((2,)),
            dma((NV // 2,)),
            dma((NV // 2,)),
        ],
    )
    return residual[None], correction[None]


def solution(mesh):
    return jax.shard_map(
        shards,
        mesh=mesh,
        in_specs=(
            P("inst", None, "space", None),
            P("inst", None, "space", None),
            P(),
            P("space"),
            P(),
            P(),
            P(),
            P(),
            P(),
        ),
        out_specs=(P("inst", None, "space", None), P("inst", None, "space", None)),
        check_vma=False,
    )
```

```python
import jax
import jax.numpy as jnp
from jax import lax
from jax.experimental import pallas as pl
from jax.experimental.pallas import tpu as pltpu
from jax.sharding import PartitionSpec as P

frequency = 0.5
viscosity = 0.01
damping = 0.25

NV = 6
NQ = 8
NS = 8
NH = 2
KB = 8
LANES = 128
LEVELS = 4


def spectral_matrix(count):
    row_index = lax.broadcasted_iota(jnp.int32, (count, count), 0)
    col_index = lax.broadcasted_iota(jnp.int32, (count, count), 1)
    distance = row_index - col_index
    parity = (1 - 2 * jnp.mod(distance, 2)).astype(jnp.float32)
    phase_angle = jnp.pi * distance.astype(jnp.float32) / count
    diagonal_mask = distance == 0
    sine_value = jnp.where(diagonal_mask, 1.0, jnp.sin(phase_angle))
    first_order = jnp.where(diagonal_mask, 0.0, 0.5 * parity * jnp.cos(phase_angle) / sine_value)
    second_order = jnp.where(
        diagonal_mask, -(count * count + 2) / 12.0, -0.5 * parity / (sine_value * sine_value)
    )
    return frequency * first_order - viscosity * second_order


def shift_chunks(tile, amount):
    sub = lax.broadcasted_iota(jnp.int32, tile.shape, 0)
    lane = lax.broadcasted_iota(jnp.int32, tile.shape, 1)
    zero = jnp.zeros_like(tile)
    swapped = pltpu.roll(tile, LANES // 2, 1)
    if amount == NQ:
        return jnp.where(lane >= LANES // 2, swapped, zero)
    if amount == -NQ:
        return jnp.where(lane < LANES // 2, swapped, zero)
    near = pltpu.roll(tile, amount % NQ, 0)
    far = pltpu.roll(swapped, amount % NQ, 0)
    if amount > 0:
        return jnp.where(sub >= amount, near, jnp.where(lane >= LANES // 2, far, zero))
    return jnp.where(sub < NQ + amount, near, jnp.where(lane < LANES // 2, far, zero))


def product(left, right):
    return [
        [sum_of([left[v][x] * right[x][w] for x in range(NV)]) for w in range(NV)]
        for v in range(NV)
    ]


def sum_of(terms):
    while len(terms) > 1:
        terms = [
            terms[i] + terms[i + 1] if i + 1 < len(terms) else terms[i]
            for i in range(0, len(terms), 2)
        ]
    return terms[0]


def applied(coef_ref, index, vector):
    return [
        sum_of([coef_ref[(v * NV + w, *index)] * vector[w] for w in range(NV)]) for v in range(NV)
    ]


def split(value):
    high = value.astype(jnp.bfloat16)
    rest = value - high.astype(jnp.float32)
    middle = rest.astype(jnp.bfloat16)
    return high, middle, (rest - middle.astype(jnp.float32)).astype(jnp.bfloat16)


def picked(select, value):
    dims = (((1,), (1,)), ((), ()))
    parts = [
        lax.dot_general(select, part, dims, preferred_element_type=jnp.float32)
        for part in split(value)
    ]
    return parts[0] + parts[1] + parts[2]


def doubled(planes):
    blank = jnp.zeros_like(planes[0])
    blocks = []
    for plane in planes:
        blocks.append(jnp.concatenate([plane, blank], axis=1))
        blocks.append(jnp.concatenate([blank, plane], axis=1))
    return jnp.concatenate(blocks, axis=0)


def fetch(pairs, sems):
    copies = [pltpu.make_async_copy(x, y, sems.at[i]) for i, (x, y) in enumerate(pairs)]
    for copy in copies:
        copy.start()
    return copies


def prepare_kernel(*refs):
    factor_ref, a_ref, up_ref, local_ref, select_ref, slope_ref, b_out, down_out = refs[9:17]
    table_ref, offset_ref, order_ref, lower_ref, upper_ref = refs[17:22]
    axial_ref, radial_ref, state_ref, forcing_ref = refs[22:26]
    b_ref, down_ref, turned_ref, sems, b_sem, down_sem = refs[26:]
    copies = fetch(list(zip(refs[:9], refs[17:26])), sems)
    for copy in copies[:5]:
        copy.wait()
    slot = lax.broadcasted_iota(jnp.int32, (LANES, LANES), 0)
    turned_ref[...] = (slot == order_ref[...]).astype(jnp.float32).T
    halves = [
        jnp.concatenate(
            [turned_ref[pl.ds(half * NS * NQ + t, NQ, stride=NS), :] for t in range(NS)], axis=0
        )
        for half in range(NH)
    ]
    select = jnp.concatenate(halves, axis=1).astype(jnp.bfloat16)
    select_ref[...] = select

    tables = [[table_ref[v * NV + w] for w in range(NV)] for v in range(NV)]
    lower = [[-lower_ref[v, w] for w in range(NV)] for v in range(NV)]
    upper = [[-upper_ref[v, w] for w in range(NV)] for v in range(NV)]
    row = lax.broadcasted_iota(jnp.int32, (NS * NQ, NH * LANES), 0)
    column = lax.broadcasted_iota(jnp.int32, (NS * NQ, NH * LANES), 1)
    place = (row % NQ) * NS + row // NQ
    place = jnp.where(column < LANES, place, place + LANES + NS * NQ)
    lines = (column == place).astype(jnp.bfloat16)
    lane = lax.broadcasted_iota(jnp.int32, (NS * NQ, LANES), 1)
    offset = jnp.concatenate([offset_ref[...], offset_ref[...]], axis=1)
    index = jnp.where(lane < LANES // 2, 0, KB) + offset
    group = LANES // (NH * KB)

    def spread(value, ref):
        planes = [e for line in value for e in line]
        padding = [jnp.zeros_like(planes[0])] * (-len(planes) % group)
        moved = picked(lines, doubled(planes + padding))
        for i in range(NV * NV):
            start = i // group * LANES
            source = moved[:, start : start + LANES]
            chosen = jnp.take_along_axis(source, index + (i % group) * NH * KB, axis=1)
            for t in range(NS):
                ref[i, t] = chosen[t * NQ : (t + 1) * NQ]

    def load(ref, t):
        return [[ref[v * NV + w, t] for w in range(NV)] for v in range(NV)]

    def keep(ref, t, value):
        for v in range(NV):
            for w in range(NV):
                ref[v * NV + w, t] = value[v][w]

    spread(product(tables, upper), b_ref)
    spread(product(tables, lower), a_ref)
    spread(tables, factor_ref)
    stores = fetch([(b_ref, b_out)], b_sem)
    keep(up_ref, 0, load(a_ref, 0))
    keep(down_ref, 0, load(b_ref, NS - 1))

    def extend(t, carry):
        keep(up_ref, 0, product(load(a_ref, t), load(up_ref, 0)))
        keep(down_ref, 0, product(load(b_ref, NS - 1 - t), load(down_ref, 0)))
        return carry

    lax.fori_loop(1, NS, extend, 0)
    for ref, sign in ((up_ref, 1), (down_ref, -1)):
        for step in range(1, LEVELS):
            level = load(ref, step - 1)
            moved = [[shift_chunks(e, sign * 2 ** (step - 1)) for e in line] for line in level]
            keep(ref, step, product(level, moved))

    stores += fetch([(down_ref, down_out)], down_sem)
    for copy in copies[5:]:
        copy.wait()
    for v in range(NV):
        for w in range(NV):
            row = jnp.full((1, LANES), 0.5 * axial_ref[v, w], jnp.float32)
            slope_ref[v * NV + w : v * NV + w + 1] = row
    stations = state_ref.shape[1]
    row = lax.broadcasted_iota(jnp.int32, (stations, LANES), 0)
    state = [state_ref[v] for v in range(NV)]
    ahead = [
        jnp.where(row == stations - 1, 0.0, pltpu.roll(state[v], stations - 1, 0))
        for v in range(NV)
    ]
    behind = [jnp.where(row == 0, 0.0, pltpu.roll(state[v], 1, 0)) for v in range(NV)]
    slope = [0.5 * (ahead[v] - behind[v]) for v in range(NV)]
    direct = [
        sum_of([axial_ref[v, w] * slope[w] for w in range(NV)])
        - damping * (ahead[v] + behind[v] - 4.0 * state[v])
        - forcing_ref[v]
        for v in range(NV)
    ]
    lines = picked(select, doubled(state))
    moved = picked(select, doubled(direct))

    def tile(array, v, t):
        return array[t * NQ : (t + 1) * NQ, v * LANES : (v + 1) * LANES]

    for t in range(NS):
        outer = [
            tile(lines, v, t + 1) if t + 1 < NS else shift_chunks(tile(lines, v, 0), -1)
            for v in range(NV)
        ]
        inner = [
            tile(lines, v, t - 1) if t > 0 else shift_chunks(tile(lines, v, NS - 1), 1)
            for v in range(NV)
        ]
        slope = [0.5 * (outer[v] - inner[v]) for v in range(NV)]
        for v in range(NV):
            local_ref[v, t] = (
                sum_of([radial_ref[v, w] * slope[w] for w in range(NV)])
                - damping * (outer[v] + inner[v])
                + tile(moved, v, t)
            )
    for copy in stores:
        copy.wait()


def time_kernel(spectral_ref, state_ref, timed_hbm, timed_ref, sem):
    count = spectral_ref.shape[0]
    rows = state_ref.shape[0] // count
    high, middle, low = split(spectral_ref[...])
    weight = jnp.concatenate([high, high, middle, high, low, middle], axis=1)
    stacked = jnp.concatenate(
        [state_ref[pl.ds(row, count, stride=rows), :] for row in range(rows)], axis=1
    )
    high, middle, low = split(stacked)
    result = jnp.dot(
        weight,
        jnp.concatenate([high, middle, high, low, high, middle], axis=0),
        preferred_element_type=jnp.float32,
    )
    for row in range(rows):
        timed_ref[pl.ds(row, count, stride=rows), :] = result[:, row * LANES : (row + 1) * LANES]
    copy = pltpu.make_async_copy(timed_ref, timed_hbm, sem)
    copy.start()
    copy.wait()


def from_lines(lines_ref, out_ref, out_hbm, sems):
    lane = lax.broadcasted_iota(jnp.int32, (LANES // 2, LANES), 1)
    half = LANES // 2
    copies = []
    for pair in range(NV // 2):
        rows = [
            lines_ref[2 * pair + p, pl.ds(sub, NS, stride=NQ), :]
            for p in range(2)
            for sub in range(NQ)
        ]
        turned = jnp.concatenate(rows, axis=0).T
        top, bottom = turned[:half], turned[half:]
        out_ref[2 * pair] = jnp.where(lane < half, top, pltpu.roll(bottom, half, 1))
        out_ref[2 * pair + 1] = jnp.where(lane < half, pltpu.roll(top, half, 1), bottom)
        both = pl.ds(2 * pair, 2)
        copies.append(pltpu.make_async_copy(out_ref.at[both], out_hbm.at[both], sems.at[pair]))
        copies[-1].start()
    return copies


def solve_kernel(*refs):
    timed_ref, select_ref, local_ref, factor_ref, a_ref, up_ref, swap_ref, other_ref = refs[:8]
    slope_ref, parity_ref, b_hbm, down_hbm, residual_hbm, correction_hbm = refs[8:14]
    joined_ref, b_ref, down_ref, residual_ref, correction_ref, lines_ref = refs[14:20]
    sems, residual_sems, correction_sems = refs[20:]
    loads = fetch([(b_hbm, b_ref), (down_hbm, down_ref)], sems)
    even = parity_ref[...] == 0.0
    high = [jnp.where(even, swap_ref[v, :1], other_ref[v, :1]) for v in range(NV)]
    low = [
        jnp.where(even, other_ref[v, 1:], swap_ref[v, 1:])
        for v in range(NV)
    ]
    row = lax.broadcasted_iota(jnp.int32, (NQ, LANES), 0)
    stations = timed_ref.shape[1]
    for v in range(NV):
        before = -sum_of([slope_ref[v * NV + w : v * NV + w + 1] * low[w] for w in range(NV)])
        after = sum_of([slope_ref[v * NV + w : v * NV + w + 1] * high[w] for w in range(NV)])
        joined_ref[v, :NQ] = timed_ref[v, :NQ] + jnp.where(row == 0, before - damping * low[v], 0.0)
        joined_ref[v, NQ : stations - NQ] = timed_ref[v, NQ : stations - NQ]
        joined_ref[v, stations - NQ :] = timed_ref[v, stations - NQ :] + jnp.where(
            row == NQ - 1, after - damping * high[v], 0.0
        )
    moved = picked(select_ref[...], doubled([joined_ref[v] for v in range(NV)]))
    own = []
    ends = None
    for t in range(NS):
        residual = []
        for v in range(NV):
            value = (
                moved[t * NQ : (t + 1) * NQ, v * LANES : (v + 1) * LANES] + local_ref[v, t]
            )
            lines_ref[v, t * NQ : (t + 1) * NQ] = value
            residual.append(value)
        value = applied(factor_ref, (t,), residual)
        own.append(value)
        if t > 0:
            value = [x + y for x, y in zip(value, applied(a_ref, (t,), ends))]
        ends = value
    copies = from_lines(lines_ref, residual_ref, residual_hbm, residual_sems)

    for step in range(LEVELS):
        more = applied(up_ref, (step,), [shift_chunks(x, 2**step) for x in ends])
        ends = [x + y for x, y in zip(ends, more)]
    carry = [shift_chunks(x, 1) for x in ends]
    sweep = []
    for t in range(NS):
        carry = [x + y for x, y in zip(own[t], applied(a_ref, (t,), carry))]
        sweep.append(carry)
    for copy in loads:
        copy.wait()
    ends = sweep[NS - 1]
    for t in reversed(range(NS - 1)):
        ends = [x + y for x, y in zip(sweep[t], applied(b_ref, (t,), ends))]
    for step in range(LEVELS):
        more = applied(down_ref, (step,), [shift_chunks(x, -(2**step)) for x in ends])
        ends = [x + y for x, y in zip(ends, more)]
    carry = [shift_chunks(x, -1) for x in ends]
    for t in reversed(range(NS)):
        carry = [x + y for x, y in zip(sweep[t], applied(b_ref, (t,), carry))]
        for v in range(NV):
            lines_ref[v, t * NQ : (t + 1) * NQ] = carry[v]
    copies += from_lines(lines_ref, correction_ref, correction_hbm, correction_sems)
    for copy in copies:
        copy.wait()


VMEM = pl.BlockSpec(memory_space=pltpu.VMEM)
MIB = 2**20
ANY = pl.BlockSpec(memory_space=pl.ANY)
PREP = 10**10


def f32(*shape):
    return jax.ShapeDtypeStruct(shape, jnp.float32)


def call(body, near, far, near_outs, far_outs, limit, flops, scratch):
    operands = [pltpu.with_memory_space_constraint(x, pltpu.VMEM) for x in near]
    operands += [pltpu.with_memory_space_constraint(x, pltpu.HBM) for x in far]
    outs = [pltpu.VMEM(x.shape, x.dtype) for x in near_outs]
    outs += [pltpu.HBM(x.shape, x.dtype) for x in far_outs]
    moved = sum(x.size * x.dtype.itemsize for x in [*near, *far, *near_outs, *far_outs])
    return pl.pallas_call(
        body,
        out_shape=outs,
        in_specs=[VMEM] * len(near) + [ANY] * len(far),
        out_specs=[VMEM] * len(near_outs) + [ANY] * len(far_outs),
        scratch_shapes=list(scratch),
        compiler_params=pltpu.CompilerParams(vmem_limit_bytes=limit * MIB),
        cost_estimate=pl.CostEstimate(flops=flops, bytes_accessed=moved, transcendentals=0),
    )(*operands)


def shards(
    flow_state,
    forcing,
    pivot_table,
    block_offset,
    line_perm,
    axial_jac,
    radial_jac,
    lower_block,
    upper_block,
):
    state = flow_state[0]
    count = lax.axis_size("inst")
    variables, stations, radial = state.shape
    share = variables * stations // count

    gathered = lax.all_to_all(
        state.reshape(count, share // 4, 4, radial), "inst", 0, 0, tiled=True
    )

    edges = state[:, :: stations - 1]
    chips = lax.axis_size("space")
    other = lax.ppermute(edges, "space", [(i, ((i + 1) ^ 1) - 1) for i in range(1, chips - 1)])
    dma = pltpu.SemaphoreType.DMA

    (timed,) = call(
        time_kernel,
        [spectral_matrix(count), gathered.reshape(count * share, radial)],
        [],
        [],
        [f32(count * share, radial)],
        8,
        2 * count * count * share * radial,
        [pltpu.VMEM((count * share, radial), jnp.float32), dma],
    )
    timed, state, edges = lax.optimization_barrier((timed, state, edges))
    swap = lax.ppermute(edges, "space", [(i, i ^ 1) for i in range(chips)])
    timed = lax.all_to_all(
        timed.reshape(count, share // 4, 4, radial), "inst", 0, 0, tiled=True
    ).reshape(variables, stations, radial)

    coef = f32(NV * NV, NS, NQ, LANES)
    level = f32(NV * NV, LEVELS, NQ, LANES)
    lines = f32(NV, NS, NQ, LANES)
    one_hot = jax.ShapeDtypeStruct((NS * NQ, NH * LANES), jnp.bfloat16)
    cells = f32(variables, stations, radial)

    def scratch(*shapes):
        return [pltpu.VMEM(x.shape, x.dtype) for x in shapes]

    inputs = [
        pivot_table.transpose(1, 2, 0, 3).reshape(NV * NV, KB, radial),
        block_offset.reshape(1, stations),
        line_perm.reshape(1, radial),
    ]
    matrices = [lower_block, upper_block, axial_jac, radial_jac]
    factor, a_table, up_table, local, select, slope, b_table, down_table = call(
        prepare_kernel,
        [],
        [*inputs, *matrices, state, forcing[0]],
        [coef, coef, level, lines, one_hot, f32(NV * NV, radial)],
        [coef, level],
        16,
        PREP,
        scratch(*inputs)
        + [pltpu.SMEM(x.shape, x.dtype) for x in matrices]
        + scratch(state, forcing[0], coef, level, f32(LANES, LANES))
        + [dma((9,)), dma((1,)), dma((1,))],
    )
    parity = jnp.full((1, radial), lax.axis_index("space") % 2, jnp.float32)
    residual, correction = call(
        solve_kernel,
        [timed, select, local, factor, a_table, up_table, swap, other, slope, parity],
        [b_table, down_table],
        [],
        [cells, cells],
        16,
        36 * 2 * 1024 * 50,
        scratch(cells, coef, level, cells, cells)
        + [
            pltpu.VMEM((NV, NS * NQ, LANES), jnp.float32),
            dma((2,)),
            dma((NV // 2,)),
            dma((NV // 2,)),
        ],
    )
    return residual[None], correction[None]


def solution(mesh):
    return jax.shard_map(
        shards,
        mesh=mesh,
        in_specs=(
            P("inst", None, "space", None),
            P("inst", None, "space", None),
            P(),
            P("space"),
            P(),
            P(),
            P(),
            P(),
            P(),
        ),
        out_specs=(P("inst", None, "space", None), P("inst", None, "space", None)),
        check_vma=False,
    )
```

```python
import jax
import jax.numpy as jnp
from jax import lax
from jax.experimental import pallas as pl
from jax.experimental.pallas import tpu as pltpu
from jax.sharding import PartitionSpec as P

frequency = 0.5
viscosity = 0.01
damping = 0.25

NV = 6
NQ = 8
NS = 8
NH = 2
KB = 8
LANES = 128
LEVELS = 4


def spectral_matrix(count):
    row_index = lax.broadcasted_iota(jnp.int32, (count, count), 0)
    col_index = lax.broadcasted_iota(jnp.int32, (count, count), 1)
    distance = row_index - col_index
    parity = (1 - 2 * jnp.mod(distance, 2)).astype(jnp.float32)
    phase_angle = jnp.pi * distance.astype(jnp.float32) / count
    diagonal_mask = distance == 0
    sine_value = jnp.where(diagonal_mask, 1.0, jnp.sin(phase_angle))
    first_order = jnp.where(diagonal_mask, 0.0, 0.5 * parity * jnp.cos(phase_angle) / sine_value)
    second_order = jnp.where(
        diagonal_mask, -(count * count + 2) / 12.0, -0.5 * parity / (sine_value * sine_value)
    )
    return frequency * first_order - viscosity * second_order


def shift_chunks(tile, amount):
    sub = lax.broadcasted_iota(jnp.int32, tile.shape, 0)
    lane = lax.broadcasted_iota(jnp.int32, tile.shape, 1)
    zero = jnp.zeros_like(tile)
    swapped = pltpu.roll(tile, LANES // 2, 1)
    if amount == NQ:
        return jnp.where(lane >= LANES // 2, swapped, zero)
    if amount == -NQ:
        return jnp.where(lane < LANES // 2, swapped, zero)
    near = pltpu.roll(tile, amount % NQ, 0)
    far = pltpu.roll(swapped, amount % NQ, 0)
    if amount > 0:
        return jnp.where(sub >= amount, near, jnp.where(lane >= LANES // 2, far, zero))
    return jnp.where(sub < NQ + amount, near, jnp.where(lane < LANES // 2, far, zero))


def product(left, right):
    return [
        [sum_of([left[v][x] * right[x][w] for x in range(NV)]) for w in range(NV)]
        for v in range(NV)
    ]


def sum_of(terms):
    while len(terms) > 1:
        terms = [
            terms[i] + terms[i + 1] if i + 1 < len(terms) else terms[i]
            for i in range(0, len(terms), 2)
        ]
    return terms[0]


def applied(coef_ref, index, vector):
    return [
        sum_of([coef_ref[(v * NV + w, *index)] * vector[w] for w in range(NV)]) for v in range(NV)
    ]


def split(value):
    high = value.astype(jnp.bfloat16)
    rest = value - high.astype(jnp.float32)
    middle = rest.astype(jnp.bfloat16)
    return high, middle, (rest - middle.astype(jnp.float32)).astype(jnp.bfloat16)


def picked(select, value):
    dims = (((1,), (1,)), ((), ()))
    parts = [
        lax.dot_general(select, part, dims, preferred_element_type=jnp.float32)
        for part in split(value)
    ]
    return parts[0] + parts[1] + parts[2]


def doubled(planes):
    blank = jnp.zeros_like(planes[0])
    blocks = []
    for plane in planes:
        blocks.append(jnp.concatenate([plane, blank], axis=1))
        blocks.append(jnp.concatenate([blank, plane], axis=1))
    return jnp.concatenate(blocks, axis=0)


def fetch(pairs, sems):
    copies = [pltpu.make_async_copy(x, y, sems.at[i]) for i, (x, y) in enumerate(pairs)]
    for copy in copies:
        copy.start()
    return copies


def edges_kernel(state_hbm, edges_ref, sems):
    last = state_hbm.shape[1] - 1
    copies = fetch(
        [(state_hbm.at[:, pl.ds(i * last, 1)], edges_ref.at[:, pl.ds(i, 1)]) for i in range(2)],
        sems,
    )
    for copy in copies:
        copy.wait()


def prepare_kernel(*refs):
    factor_ref, a_ref, up_ref, local_ref, select_ref, slope_ref, b_out, down_out = refs[9:17]
    table_ref, offset_ref, order_ref, lower_ref, upper_ref = refs[17:22]
    axial_ref, radial_ref, state_ref, forcing_ref = refs[22:26]
    b_ref, down_ref, turned_ref, sems, b_sem, down_sem = refs[26:]
    copies = fetch(list(zip(refs[:9], refs[17:26])), sems)
    for copy in copies[:5]:
        copy.wait()
    slot = lax.broadcasted_iota(jnp.int32, (LANES, LANES), 0)
    turned_ref[...] = (slot == order_ref[...]).astype(jnp.float32).T
    halves = [
        jnp.concatenate(
            [turned_ref[pl.ds(half * NS * NQ + t, NQ, stride=NS), :] for t in range(NS)], axis=0
        )
        for half in range(NH)
    ]
    select = jnp.concatenate(halves, axis=1).astype(jnp.bfloat16)
    select_ref[...] = select

    tables = [[table_ref[v * NV + w] for w in range(NV)] for v in range(NV)]
    lower = [[-lower_ref[v, w] for w in range(NV)] for v in range(NV)]
    upper = [[-upper_ref[v, w] for w in range(NV)] for v in range(NV)]
    row = lax.broadcasted_iota(jnp.int32, (NS * NQ, NH * LANES), 0)
    column = lax.broadcasted_iota(jnp.int32, (NS * NQ, NH * LANES), 1)
    place = (row % NQ) * NS + row // NQ
    place = jnp.where(column < LANES, place, place + LANES + NS * NQ)
    lines = (column == place).astype(jnp.bfloat16)
    lane = lax.broadcasted_iota(jnp.int32, (NS * NQ, LANES), 1)
    offset = jnp.concatenate([offset_ref[...], offset_ref[...]], axis=1)
    index = jnp.where(lane < LANES // 2, 0, KB) + offset
    group = LANES // (NH * KB)

    def spread(value, ref):
        planes = [e for line in value for e in line]
        padding = [jnp.zeros_like(planes[0])] * (-len(planes) % group)
        moved = picked(lines, doubled(planes + padding))
        for i in range(NV * NV):
            start = i // group * LANES
            source = moved[:, start : start + LANES]
            chosen = jnp.take_along_axis(source, index + (i % group) * NH * KB, axis=1)
            for t in range(NS):
                ref[i, t] = chosen[t * NQ : (t + 1) * NQ]

    def load(ref, t):
        return [[ref[v * NV + w, t] for w in range(NV)] for v in range(NV)]

    def keep(ref, t, value):
        for v in range(NV):
            for w in range(NV):
                ref[v * NV + w, t] = value[v][w]

    spread(product(tables, upper), b_ref)
    spread(product(tables, lower), a_ref)
    spread(tables, factor_ref)
    stores = fetch([(b_ref, b_out)], b_sem)
    keep(up_ref, 0, load(a_ref, 0))
    keep(down_ref, 0, load(b_ref, NS - 1))

    def extend(t, carry):
        keep(up_ref, 0, product(load(a_ref, t), load(up_ref, 0)))
        keep(down_ref, 0, product(load(b_ref, NS - 1 - t), load(down_ref, 0)))
        return carry

    lax.fori_loop(1, NS, extend, 0)
    for ref, sign in ((up_ref, 1), (down_ref, -1)):
        for step in range(1, LEVELS):
            level = load(ref, step - 1)
            moved = [[shift_chunks(e, sign * 2 ** (step - 1)) for e in line] for line in level]
            keep(ref, step, product(level, moved))

    stores += fetch([(down_ref, down_out)], down_sem)
    for copy in copies[5:]:
        copy.wait()
    for v in range(NV):
        for w in range(NV):
            row = jnp.full((1, LANES), 0.5 * axial_ref[v, w], jnp.float32)
            slope_ref[v * NV + w : v * NV + w + 1] = row
    stations = state_ref.shape[1]
    row = lax.broadcasted_iota(jnp.int32, (stations, LANES), 0)
    state = [state_ref[v] for v in range(NV)]
    ahead = [
        jnp.where(row == stations - 1, 0.0, pltpu.roll(state[v], stations - 1, 0))
        for v in range(NV)
    ]
    behind = [jnp.where(row == 0, 0.0, pltpu.roll(state[v], 1, 0)) for v in range(NV)]
    slope = [0.5 * (ahead[v] - behind[v]) for v in range(NV)]
    direct = [
        sum_of([axial_ref[v, w] * slope[w] for w in range(NV)])
        - damping * (ahead[v] + behind[v] - 4.0 * state[v])
        - forcing_ref[v]
        for v in range(NV)
    ]
    lines = picked(select, doubled(state))
    moved = picked(select, doubled(direct))

    def tile(array, v, t):
        return array[t * NQ : (t + 1) * NQ, v * LANES : (v + 1) * LANES]

    for t in range(NS):
        outer = [
            tile(lines, v, t + 1) if t + 1 < NS else shift_chunks(tile(lines, v, 0), -1)
            for v in range(NV)
        ]
        inner = [
            tile(lines, v, t - 1) if t > 0 else shift_chunks(tile(lines, v, NS - 1), 1)
            for v in range(NV)
        ]
        slope = [0.5 * (outer[v] - inner[v]) for v in range(NV)]
        for v in range(NV):
            local_ref[v, t] = (
                sum_of([radial_ref[v, w] * slope[w] for w in range(NV)])
                - damping * (outer[v] + inner[v])
                + tile(moved, v, t)
            )
    for copy in stores:
        copy.wait()


def time_kernel(spectral_ref, state_ref, timed_hbm, timed_ref, sem):
    count = spectral_ref.shape[0]
    rows = state_ref.shape[0] // count
    high, middle, low = split(spectral_ref[...])
    weight = jnp.concatenate([high, high, middle, high, low, middle], axis=1)
    stacked = jnp.concatenate(
        [state_ref[pl.ds(row, count, stride=rows), :] for row in range(rows)], axis=1
    )
    high, middle, low = split(stacked)
    result = jnp.dot(
        weight,
        jnp.concatenate([high, middle, high, low, high, middle], axis=0),
        preferred_element_type=jnp.float32,
    )
    for row in range(rows):
        timed_ref[pl.ds(row, count, stride=rows), :] = result[:, row * LANES : (row + 1) * LANES]
    copy = pltpu.make_async_copy(timed_ref, timed_hbm, sem)
    copy.start()
    copy.wait()


def from_lines(lines_ref, out_ref, out_hbm, sems):
    lane = lax.broadcasted_iota(jnp.int32, (LANES // 2, LANES), 1)
    half = LANES // 2
    copies = []
    for pair in range(NV // 2):
        rows = [
            lines_ref[2 * pair + p, pl.ds(sub, NS, stride=NQ), :]
            for p in range(2)
            for sub in range(NQ)
        ]
        turned = jnp.concatenate(rows, axis=0).T
        top, bottom = turned[:half], turned[half:]
        out_ref[2 * pair] = jnp.where(lane < half, top, pltpu.roll(bottom, half, 1))
        out_ref[2 * pair + 1] = jnp.where(lane < half, pltpu.roll(top, half, 1), bottom)
        both = pl.ds(2 * pair, 2)
        copies.append(pltpu.make_async_copy(out_ref.at[both], out_hbm.at[both], sems.at[pair]))
        copies[-1].start()
    return copies


def solve_kernel(*refs):
    timed_ref, select_ref, local_ref, factor_ref, a_ref, up_ref, swap_ref, other_ref = refs[:8]
    slope_ref, parity_ref, b_hbm, down_hbm, residual_hbm, correction_hbm = refs[8:14]
    joined_ref, b_ref, down_ref, residual_ref, correction_ref, lines_ref = refs[14:20]
    sems, residual_sems, correction_sems = refs[20:]
    loads = fetch([(b_hbm, b_ref), (down_hbm, down_ref)], sems)
    even = parity_ref[...] == 0.0
    high = [jnp.where(even, swap_ref[v, :1], other_ref[v, :1]) for v in range(NV)]
    low = [
        jnp.where(even, other_ref[v, 1:], swap_ref[v, 1:])
        for v in range(NV)
    ]
    row = lax.broadcasted_iota(jnp.int32, (NQ, LANES), 0)
    stations = timed_ref.shape[1]
    for v in range(NV):
        before = -sum_of([slope_ref[v * NV + w : v * NV + w + 1] * low[w] for w in range(NV)])
        after = sum_of([slope_ref[v * NV + w : v * NV + w + 1] * high[w] for w in range(NV)])
        joined_ref[v, :NQ] = timed_ref[v, :NQ] + jnp.where(row == 0, before - damping * low[v], 0.0)
        joined_ref[v, NQ : stations - NQ] = timed_ref[v, NQ : stations - NQ]
        joined_ref[v, stations - NQ :] = timed_ref[v, stations - NQ :] + jnp.where(
            row == NQ - 1, after - damping * high[v], 0.0
        )
    moved = picked(select_ref[...], doubled([joined_ref[v] for v in range(NV)]))
    own = []
    ends = None
    for t in range(NS):
        residual = []
        for v in range(NV):
            value = (
                moved[t * NQ : (t + 1) * NQ, v * LANES : (v + 1) * LANES] + local_ref[v, t]
            )
            lines_ref[v, t * NQ : (t + 1) * NQ] = value
            residual.append(value)
        value = applied(factor_ref, (t,), residual)
        own.append(value)
        if t > 0:
            value = [x + y for x, y in zip(value, applied(a_ref, (t,), ends))]
        ends = value
    copies = from_lines(lines_ref, residual_ref, residual_hbm, residual_sems)

    for step in range(LEVELS):
        more = applied(up_ref, (step,), [shift_chunks(x, 2**step) for x in ends])
        ends = [x + y for x, y in zip(ends, more)]
    carry = [shift_chunks(x, 1) for x in ends]
    sweep = []
    for t in range(NS):
        carry = [x + y for x, y in zip(own[t], applied(a_ref, (t,), carry))]
        sweep.append(carry)
    loads[0].wait()
    ends = sweep[NS - 1]
    for t in reversed(range(NS - 1)):
        ends = [x + y for x, y in zip(sweep[t], applied(b_ref, (t,), ends))]
    loads[1].wait()
    for step in range(LEVELS):
        more = applied(down_ref, (step,), [shift_chunks(x, -(2**step)) for x in ends])
        ends = [x + y for x, y in zip(ends, more)]
    carry = [shift_chunks(x, -1) for x in ends]
    for t in reversed(range(NS)):
        carry = [x + y for x, y in zip(sweep[t], applied(b_ref, (t,), carry))]
        for v in range(NV):
            lines_ref[v, t * NQ : (t + 1) * NQ] = carry[v]
    copies += from_lines(lines_ref, correction_ref, correction_hbm, correction_sems)
    for copy in copies:
        copy.wait()


VMEM = pl.BlockSpec(memory_space=pltpu.VMEM)
MIB = 2**20
ANY = pl.BlockSpec(memory_space=pl.ANY)
PREP = 10**10


def f32(*shape):
    return jax.ShapeDtypeStruct(shape, jnp.float32)


def call(body, near, far, near_outs, far_outs, limit, flops, scratch):
    operands = [pltpu.with_memory_space_constraint(x, pltpu.VMEM) for x in near]
    operands += [pltpu.with_memory_space_constraint(x, pltpu.HBM) for x in far]
    outs = [pltpu.VMEM(x.shape, x.dtype) for x in near_outs]
    outs += [pltpu.HBM(x.shape, x.dtype) for x in far_outs]
    moved = sum(x.size * x.dtype.itemsize for x in [*near, *far, *near_outs, *far_outs])
    return pl.pallas_call(
        body,
        out_shape=outs,
        in_specs=[VMEM] * len(near) + [ANY] * len(far),
        out_specs=[VMEM] * len(near_outs) + [ANY] * len(far_outs),
        scratch_shapes=list(scratch),
        compiler_params=pltpu.CompilerParams(vmem_limit_bytes=limit * MIB),
        cost_estimate=pl.CostEstimate(flops=flops, bytes_accessed=moved, transcendentals=0),
    )(*operands)


def shards(
    flow_state,
    forcing,
    pivot_table,
    block_offset,
    line_perm,
    axial_jac,
    radial_jac,
    lower_block,
    upper_block,
):
    state = flow_state[0]
    count = lax.axis_size("inst")
    variables, stations, radial = state.shape
    share = variables * stations // count

    gathered = lax.all_to_all(
        state.reshape(count, share // 4, 4, radial), "inst", 0, 0, tiled=True
    )

    dma = pltpu.SemaphoreType.DMA
    (edges,) = call(
        edges_kernel,
        [],
        [state],
        [f32(variables, 2, radial)],
        [],
        4,
        1,
        [dma((2,))],
    )
    chips = lax.axis_size("space")
    other = lax.ppermute(edges, "space", [(i, ((i + 1) ^ 1) - 1) for i in range(1, chips - 1)])

    (timed,) = call(
        time_kernel,
        [spectral_matrix(count), gathered.reshape(count * share, radial)],
        [],
        [],
        [f32(count * share, radial)],
        8,
        2 * count * count * share * radial,
        [pltpu.VMEM((count * share, radial), jnp.float32), dma],
    )
    timed, state, edges = lax.optimization_barrier((timed, state, edges))
    swap = lax.ppermute(edges, "space", [(i, i ^ 1) for i in range(chips)])
    timed = lax.all_to_all(
        timed.reshape(count, share // 4, 4, radial), "inst", 0, 0, tiled=True
    ).reshape(variables, stations, radial)

    coef = f32(NV * NV, NS, NQ, LANES)
    level = f32(NV * NV, LEVELS, NQ, LANES)
    lines = f32(NV, NS, NQ, LANES)
    one_hot = jax.ShapeDtypeStruct((NS * NQ, NH * LANES), jnp.bfloat16)
    cells = f32(variables, stations, radial)

    def scratch(*shapes):
        return [pltpu.VMEM(x.shape, x.dtype) for x in shapes]

    inputs = [
        pivot_table.transpose(1, 2, 0, 3).reshape(NV * NV, KB, radial),
        block_offset.reshape(1, stations),
        line_perm.reshape(1, radial),
    ]
    matrices = [lower_block, upper_block, axial_jac, radial_jac]
    factor, a_table, up_table, local, select, slope, b_table, down_table = call(
        prepare_kernel,
        [],
        [*inputs, *matrices, state, forcing[0]],
        [coef, coef, level, lines, one_hot, f32(NV * NV, radial)],
        [coef, level],
        16,
        PREP,
        scratch(*inputs)
        + [pltpu.SMEM(x.shape, x.dtype) for x in matrices]
        + scratch(state, forcing[0], coef, level, f32(LANES, LANES))
        + [dma((9,)), dma((1,)), dma((1,))],
    )
    parity = jnp.full((1, radial), lax.axis_index("space") % 2, jnp.float32)
    residual, correction = call(
        solve_kernel,
        [timed, select, local, factor, a_table, up_table, swap, other, slope, parity],
        [b_table, down_table],
        [],
        [cells, cells],
        16,
        36 * 2 * 1024 * 50,
        scratch(cells, coef, level, cells, cells)
        + [
            pltpu.VMEM((NV, NS * NQ, LANES), jnp.float32),
            dma((2,)),
            dma((NV // 2,)),
            dma((NV // 2,)),
        ],
    )
    return residual[None], correction[None]


def solution(mesh):
    return jax.shard_map(
        shards,
        mesh=mesh,
        in_specs=(
            P("inst", None, "space", None),
            P("inst", None, "space", None),
            P(),
            P("space"),
            P(),
            P(),
            P(),
            P(),
            P(),
        ),
        out_specs=(P("inst", None, "space", None), P("inst", None, "space", None)),
        check_vma=False,
    )
```

```python
import jax
import jax.numpy as jnp
import numpy as np
from jax import lax
from jax.experimental import pallas as pl
from jax.experimental.pallas import tpu as pltpu
from jax.sharding import PartitionSpec as P

frequency = 0.5
viscosity = 0.01
damping = 0.25

NV = 6
NQ = 8
NS = 8
NH = 2
KB = 8
LANES = 128
LEVELS = 4


def spectral_weight(count):
    distance = np.arange(count)[:, None] - np.arange(count)[None]
    parity = 1.0 - 2.0 * (distance % 2)
    angle = np.pi * distance / count
    diagonal = distance == 0
    sine = np.where(diagonal, 1.0, np.sin(angle))
    first = np.where(diagonal, 0.0, 0.5 * parity * np.cos(angle) / sine)
    second = np.where(diagonal, -(count * count + 2) / 12.0, -0.5 * parity / (sine * sine))
    rest = (frequency * first - viscosity * second).astype(np.float32)
    parts = []
    for _ in range(3):
        parts.append(rest.astype(jnp.bfloat16))
        rest = rest - parts[-1].astype(np.float32)
    high, middle, low = parts
    return np.concatenate([high, high, middle, high, low, middle], axis=1)


def shift_chunks(tile, amount):
    sub = lax.broadcasted_iota(jnp.int32, tile.shape, 0)
    lane = lax.broadcasted_iota(jnp.int32, tile.shape, 1)
    zero = jnp.zeros_like(tile)
    swapped = pltpu.roll(tile, LANES // 2, 1)
    if amount == NQ:
        return jnp.where(lane >= LANES // 2, swapped, zero)
    if amount == -NQ:
        return jnp.where(lane < LANES // 2, swapped, zero)
    near = pltpu.roll(tile, amount % NQ, 0)
    far = pltpu.roll(swapped, amount % NQ, 0)
    if amount > 0:
        return jnp.where(sub >= amount, near, jnp.where(lane >= LANES // 2, far, zero))
    return jnp.where(sub < NQ + amount, near, jnp.where(lane < LANES // 2, far, zero))


def product(left, right):
    return [
        [sum_of([left[v][x] * right[x][w] for x in range(NV)]) for w in range(NV)]
        for v in range(NV)
    ]


def sum_of(terms):
    while len(terms) > 1:
        terms = [
            terms[i] + terms[i + 1] if i + 1 < len(terms) else terms[i]
            for i in range(0, len(terms), 2)
        ]
    return terms[0]


def applied(coef_ref, index, vector):
    return [
        sum_of([coef_ref[(v * NV + w, *index)] * vector[w] for w in range(NV)]) for v in range(NV)
    ]


def split(value):
    high = value.astype(jnp.bfloat16)
    rest = value - high.astype(jnp.float32)
    middle = rest.astype(jnp.bfloat16)
    return high, middle, (rest - middle.astype(jnp.float32)).astype(jnp.bfloat16)


def picked(select, value):
    dims = (((1,), (1,)), ((), ()))
    parts = [
        lax.dot_general(select, part, dims, preferred_element_type=jnp.float32)
        for part in split(value)
    ]
    return parts[0] + parts[1] + parts[2]


def doubled(planes):
    blank = jnp.zeros_like(planes[0])
    blocks = []
    for plane in planes:
        blocks.append(jnp.concatenate([plane, blank], axis=1))
        blocks.append(jnp.concatenate([blank, plane], axis=1))
    return jnp.concatenate(blocks, axis=0)


def fetch(pairs, sems):
    copies = [pltpu.make_async_copy(x, y, sems.at[i]) for i, (x, y) in enumerate(pairs)]
    for copy in copies:
        copy.start()
    return copies


def edges_kernel(state_hbm, weight_hbm, edges_ref, weight_ref, sems):
    last = state_hbm.shape[1] - 1
    pairs = [(state_hbm.at[:, pl.ds(i * last, 1)], edges_ref.at[:, pl.ds(i, 1)]) for i in range(2)]
    for copy in fetch([*pairs, (weight_hbm, weight_ref)], sems):
        copy.wait()


def prepare_kernel(*refs):
    factor_ref, a_ref, up_ref, local_ref, select_ref, slope_ref, b_out, down_out = refs[9:17]
    table_ref, offset_ref, order_ref, lower_ref, upper_ref = refs[17:22]
    axial_ref, radial_ref, state_ref, forcing_ref = refs[22:26]
    b_ref, down_ref, turned_ref, sems, b_sem, down_sem = refs[26:]
    copies = fetch(list(zip(refs[:9], refs[17:26])), sems)
    for copy in copies[:5]:
        copy.wait()
    slot = lax.broadcasted_iota(jnp.int32, (LANES, LANES), 0)
    turned_ref[...] = (slot == order_ref[...]).astype(jnp.float32).T
    halves = [
        jnp.concatenate(
            [turned_ref[pl.ds(half * NS * NQ + t, NQ, stride=NS), :] for t in range(NS)], axis=0
        )
        for half in range(NH)
    ]
    select = jnp.concatenate(halves, axis=1).astype(jnp.bfloat16)
    select_ref[...] = select

    tables = [[table_ref[v * NV + w] for w in range(NV)] for v in range(NV)]
    lower = [[-lower_ref[v, w] for w in range(NV)] for v in range(NV)]
    upper = [[-upper_ref[v, w] for w in range(NV)] for v in range(NV)]
    row = lax.broadcasted_iota(jnp.int32, (NS * NQ, NH * LANES), 0)
    column = lax.broadcasted_iota(jnp.int32, (NS * NQ, NH * LANES), 1)
    place = (row % NQ) * NS + row // NQ
    place = jnp.where(column < LANES, place, place + LANES + NS * NQ)
    lines = (column == place).astype(jnp.bfloat16)
    lane = lax.broadcasted_iota(jnp.int32, (NS * NQ, LANES), 1)
    offset = jnp.concatenate([offset_ref[...], offset_ref[...]], axis=1)
    index = jnp.where(lane < LANES // 2, 0, KB) + offset
    group = LANES // (NH * KB)

    def spread(value, ref):
        planes = [e for line in value for e in line]
        padding = [jnp.zeros_like(planes[0])] * (-len(planes) % group)
        moved = picked(lines, doubled(planes + padding))
        for i in range(NV * NV):
            start = i // group * LANES
            source = moved[:, start : start + LANES]
            chosen = jnp.take_along_axis(source, index + (i % group) * NH * KB, axis=1)
            for t in range(NS):
                ref[i, t] = chosen[t * NQ : (t + 1) * NQ]

    def load(ref, t):
        return [[ref[v * NV + w, t] for w in range(NV)] for v in range(NV)]

    def keep(ref, t, value):
        for v in range(NV):
            for w in range(NV):
                ref[v * NV + w, t] = value[v][w]

    spread(product(tables, upper), b_ref)
    spread(product(tables, lower), a_ref)
    spread(tables, factor_ref)
    stores = fetch([(b_ref, b_out)], b_sem)
    keep(up_ref, 0, load(a_ref, 0))
    keep(down_ref, 0, load(b_ref, NS - 1))

    def extend(t, carry):
        keep(up_ref, 0, product(load(a_ref, t), load(up_ref, 0)))
        keep(down_ref, 0, product(load(b_ref, NS - 1 - t), load(down_ref, 0)))
        return carry

    for t in range(1, NS):
        extend(t, 0)
    for ref, sign in ((up_ref, 1), (down_ref, -1)):
        for step in range(1, LEVELS):
            level = load(ref, step - 1)
            moved = [[shift_chunks(e, sign * 2 ** (step - 1)) for e in line] for line in level]
            keep(ref, step, product(level, moved))

    stores += fetch([(down_ref, down_out)], down_sem)
    for copy in copies[5:]:
        copy.wait()
    for v in range(NV):
        for w in range(NV):
            row = jnp.full((1, LANES), 0.5 * axial_ref[v, w], jnp.float32)
            slope_ref[v * NV + w : v * NV + w + 1] = row
    stations = state_ref.shape[1]
    row = lax.broadcasted_iota(jnp.int32, (stations, LANES), 0)
    state = [state_ref[v] for v in range(NV)]
    ahead = [
        jnp.where(row == stations - 1, 0.0, pltpu.roll(state[v], stations - 1, 0))
        for v in range(NV)
    ]
    behind = [jnp.where(row == 0, 0.0, pltpu.roll(state[v], 1, 0)) for v in range(NV)]
    slope = [0.5 * (ahead[v] - behind[v]) for v in range(NV)]
    direct = [
        sum_of([axial_ref[v, w] * slope[w] for w in range(NV)])
        - damping * (ahead[v] + behind[v] - 4.0 * state[v])
        - forcing_ref[v]
        for v in range(NV)
    ]
    lines = picked(select, doubled(state))
    moved = picked(select, doubled(direct))

    def tile(array, v, t):
        return array[t * NQ : (t + 1) * NQ, v * LANES : (v + 1) * LANES]

    for t in range(NS):
        outer = [
            tile(lines, v, t + 1) if t + 1 < NS else shift_chunks(tile(lines, v, 0), -1)
            for v in range(NV)
        ]
        inner = [
            tile(lines, v, t - 1) if t > 0 else shift_chunks(tile(lines, v, NS - 1), 1)
            for v in range(NV)
        ]
        slope = [0.5 * (outer[v] - inner[v]) for v in range(NV)]
        for v in range(NV):
            local_ref[v, t] = (
                sum_of([radial_ref[v, w] * slope[w] for w in range(NV)])
                - damping * (outer[v] + inner[v])
                + tile(moved, v, t)
            )
    for copy in stores:
        copy.wait()


def time_kernel(weight_ref, state_ref, timed_hbm, timed_ref, sem):
    count = weight_ref.shape[0]
    rows = state_ref.shape[0] // count
    stacked = jnp.concatenate(
        [state_ref[pl.ds(row, count, stride=rows), :] for row in range(rows)], axis=1
    )
    high, middle, low = split(stacked)
    result = jnp.dot(
        weight_ref[...],
        jnp.concatenate([high, middle, high, low, high, middle], axis=0),
        preferred_element_type=jnp.float32,
    )
    for row in range(rows):
        timed_ref[pl.ds(row, count, stride=rows), :] = result[:, row * LANES : (row + 1) * LANES]
    copy = pltpu.make_async_copy(timed_ref, timed_hbm, sem)
    copy.start()
    copy.wait()


def from_lines(lines_ref, out_ref, pair):
    lane = lax.broadcasted_iota(jnp.int32, (LANES // 2, LANES), 1)
    half = LANES // 2
    rows = [
        lines_ref[2 * pair + p, pl.ds(sub, NS, stride=NQ), :]
        for p in range(2)
        for sub in range(NQ)
    ]
    turned = jnp.concatenate(rows, axis=0).T
    top, bottom = turned[:half], turned[half:]
    out_ref[2 * pair] = jnp.where(lane < half, top, pltpu.roll(bottom, half, 1))
    out_ref[2 * pair + 1] = jnp.where(lane < half, pltpu.roll(top, half, 1), bottom)


def solve_kernel(*refs):
    timed_ref, select_ref, local_ref, factor_ref, a_ref, up_ref, swap_ref, other_ref = refs[:8]
    slope_ref, parity_ref, b_hbm, down_hbm, residual_hbm, correction_hbm = refs[8:14]
    joined_ref, b_ref, down_ref, residual_ref, correction_ref, lines_ref = refs[14:20]
    sems, residual_sem, correction_sems = refs[20:]
    loads = fetch([(b_hbm, b_ref), (down_hbm, down_ref)], sems)
    even = parity_ref[...] == 0.0
    high = [jnp.where(even, swap_ref[v, :1], other_ref[v, :1]) for v in range(NV)]
    low = [
        jnp.where(even, other_ref[v, 1:], swap_ref[v, 1:])
        for v in range(NV)
    ]
    row = lax.broadcasted_iota(jnp.int32, (NQ, LANES), 0)
    stations = timed_ref.shape[1]
    for v in range(NV):
        before = -sum_of([slope_ref[v * NV + w : v * NV + w + 1] * low[w] for w in range(NV)])
        after = sum_of([slope_ref[v * NV + w : v * NV + w + 1] * high[w] for w in range(NV)])
        joined_ref[v, :NQ] = timed_ref[v, :NQ] + jnp.where(row == 0, before - damping * low[v], 0.0)
        joined_ref[v, NQ : stations - NQ] = timed_ref[v, NQ : stations - NQ]
        joined_ref[v, stations - NQ :] = timed_ref[v, stations - NQ :] + jnp.where(
            row == NQ - 1, after - damping * high[v], 0.0
        )
    moved = picked(select_ref[...], doubled([joined_ref[v] for v in range(NV)]))
    own = []
    ends = None
    for t in range(NS):
        residual = []
        for v in range(NV):
            value = (
                moved[t * NQ : (t + 1) * NQ, v * LANES : (v + 1) * LANES] + local_ref[v, t]
            )
            lines_ref[v, t * NQ : (t + 1) * NQ] = value
            residual.append(value)
        value = applied(factor_ref, (t,), residual)
        own.append(value)
        if t > 0:
            value = [x + y for x, y in zip(value, applied(a_ref, (t,), ends))]
        ends = value
    for pair in range(NV // 2):
        from_lines(lines_ref, residual_ref, pair)

    for step in range(LEVELS):
        more = applied(up_ref, (step,), [shift_chunks(x, 2**step) for x in ends])
        ends = [x + y for x, y in zip(ends, more)]
    carry = [shift_chunks(x, 1) for x in ends]
    sweep = []
    for t in range(NS):
        carry = [x + y for x, y in zip(own[t], applied(a_ref, (t,), carry))]
        sweep.append(carry)
    copies = fetch([(residual_ref, residual_hbm)], residual_sem)
    loads[0].wait()
    ends = sweep[NS - 1]
    for t in reversed(range(NS - 1)):
        ends = [x + y for x, y in zip(sweep[t], applied(b_ref, (t,), ends))]
    loads[1].wait()
    for step in range(LEVELS):
        more = applied(down_ref, (step,), [shift_chunks(x, -(2**step)) for x in ends])
        ends = [x + y for x, y in zip(ends, more)]
    carry = [shift_chunks(x, -1) for x in ends]
    for t in reversed(range(NS)):
        carry = [x + y for x, y in zip(sweep[t], applied(b_ref, (t,), carry))]
        for v in range(NV):
            lines_ref[v, t * NQ : (t + 1) * NQ] = carry[v]
    for pair in range(NV // 2):
        from_lines(lines_ref, correction_ref, pair)
        both = pl.ds(2 * pair, 2)
        copies.append(
            pltpu.make_async_copy(
                correction_ref.at[both], correction_hbm.at[both], correction_sems.at[pair]
            )
        )
        copies[-1].start()
    for copy in copies:
        copy.wait()


VMEM = pl.BlockSpec(memory_space=pltpu.VMEM)
MIB = 2**20
ANY = pl.BlockSpec(memory_space=pl.ANY)
PREP = 10**10


def f32(*shape):
    return jax.ShapeDtypeStruct(shape, jnp.float32)


def call(body, near, far, near_outs, far_outs, limit, flops, scratch):
    operands = [pltpu.with_memory_space_constraint(x, pltpu.VMEM) for x in near]
    operands += [pltpu.with_memory_space_constraint(x, pltpu.HBM) for x in far]
    outs = [pltpu.VMEM(x.shape, x.dtype) for x in near_outs]
    outs += [pltpu.HBM(x.shape, x.dtype) for x in far_outs]
    moved = sum(x.size * x.dtype.itemsize for x in [*near, *far, *near_outs, *far_outs])
    return pl.pallas_call(
        body,
        out_shape=outs,
        in_specs=[VMEM] * len(near) + [ANY] * len(far),
        out_specs=[VMEM] * len(near_outs) + [ANY] * len(far_outs),
        scratch_shapes=list(scratch),
        compiler_params=pltpu.CompilerParams(vmem_limit_bytes=limit * MIB),
        cost_estimate=pl.CostEstimate(flops=flops, bytes_accessed=moved, transcendentals=0),
    )(*operands)


def shards(
    flow_state,
    forcing,
    pivot_table,
    block_offset,
    line_perm,
    axial_jac,
    radial_jac,
    lower_block,
    upper_block,
):
    state = flow_state[0]
    count = lax.axis_size("inst")
    variables, stations, radial = state.shape
    share = variables * stations // count

    gathered = lax.all_to_all(
        state.reshape(count, share // 4, 4, radial), "inst", 0, 0, tiled=True
    )

    dma = pltpu.SemaphoreType.DMA
    weight = jnp.asarray(spectral_weight(count))
    edges, weight = call(
        edges_kernel,
        [],
        [state, weight],
        [f32(variables, 2, radial), weight],
        [],
        4,
        1,
        [dma((3,))],
    )
    chips = lax.axis_size("space")
    other = lax.ppermute(edges, "space", [(i, ((i + 1) ^ 1) - 1) for i in range(1, chips - 1)])

    (timed,) = call(
        time_kernel,
        [weight, gathered.reshape(count * share, radial)],
        [],
        [],
        [f32(count * share, radial)],
        8,
        2 * count * count * share * radial,
        [pltpu.VMEM((count * share, radial), jnp.float32), dma],
    )
    timed, state, edges = lax.optimization_barrier((timed, state, edges))
    swap = lax.ppermute(edges, "space", [(i, i ^ 1) for i in range(chips)])
    timed = lax.all_to_all(
        timed.reshape(count, share // 4, 4, radial), "inst", 0, 0, tiled=True
    ).reshape(variables, stations, radial)

    coef = f32(NV * NV, NS, NQ, LANES)
    level = f32(NV * NV, LEVELS, NQ, LANES)
    lines = f32(NV, NS, NQ, LANES)
    one_hot = jax.ShapeDtypeStruct((NS * NQ, NH * LANES), jnp.bfloat16)
    cells = f32(variables, stations, radial)

    def scratch(*shapes):
        return [pltpu.VMEM(x.shape, x.dtype) for x in shapes]

    inputs = [
        pivot_table.transpose(1, 2, 0, 3).reshape(NV * NV, KB, radial),
        block_offset.reshape(1, stations),
        line_perm.reshape(1, radial),
    ]
    matrices = [lower_block, upper_block, axial_jac, radial_jac]
    factor, a_table, up_table, local, select, slope, b_table, down_table = call(
        prepare_kernel,
        [],
        [*inputs, *matrices, state, forcing[0]],
        [coef, coef, level, lines, one_hot, f32(NV * NV, radial)],
        [coef, level],
        16,
        PREP,
        scratch(*inputs)
        + [pltpu.SMEM(x.shape, x.dtype) for x in matrices]
        + scratch(state, forcing[0], coef, level, f32(LANES, LANES))
        + [dma((9,)), dma((1,)), dma((1,))],
    )
    parity = jnp.full((1, radial), lax.axis_index("space") % 2, jnp.float32)
    residual, correction = call(
        solve_kernel,
        [timed, select, local, factor, a_table, up_table, swap, other, slope, parity],
        [b_table, down_table],
        [],
        [cells, cells],
        16,
        36 * 2 * 1024 * 50,
        scratch(cells, coef, level, cells, cells)
        + [
            pltpu.VMEM((NV, NS * NQ, LANES), jnp.float32),
            dma((2,)),
            dma((1,)),
            dma((NV // 2,)),
        ],
    )
    return residual[None], correction[None]


def solution(mesh):
    return jax.shard_map(
        shards,
        mesh=mesh,
        in_specs=(
            P("inst", None, "space", None),
            P("inst", None, "space", None),
            P(),
            P("space"),
            P(),
            P(),
            P(),
            P(),
            P(),
        ),
        out_specs=(P("inst", None, "space", None), P("inst", None, "space", None)),
        check_vma=False,
    )
```
